256 devices in a mesh: space: 128 (over y, z, x), tm: 2 (over core).
Axes of the slice: x: 4, y: 4, z: 8, core: 2. Of those that a mesh axis runs over, the one named last changes fastest.
Arguments:
- snapshots: bfloat16 [2097152, 512], P(('space', 'tm')), may hold values from -6 to 6
- range_test: bfloat16 [512, 128], replicated, may hold values from -0.25 to 0.25
- test_rows: bfloat16 [256, 2097152], P(None, ('space', 'tm')), may hold values from -0.00390625 to 0.00390625
- species: int32 [2048, 1024], P(('space', 'tm')), may hold values from 0 to 3
- reaction_rates: float32 [4], replicated, may hold values from 1 to 8
- adjoint_end: float32 [2048, 1024], P(('space', 'tm')), may hold values from -6 to 6
Outputs:
- adjoint: float32 [2048, 1024], P(('space', 'tm'))
- time_factors: float32 [128, 512], P(None, ('space', 'tm'))
The draws below stay inside these ranges and needn't reach their ends.
All inputs are finite; a program needn't handle non-finite values.
Results may differ from the reference program's by a relative error of at most 0.0012.
Values sent between devices are 32-bit elements; how exact they have to be, the bound alone decides.
A program may use at most 64 MiB of HBM per device.

```python
import math
import jax
import jax.numpy as jnp
from jax import lax

GY = 1024
TIMES = 512
RANK = 128
SKETCH = 256
SPECIES = 4
NX = 2048
CELLS = 2097152


def set_ends(entries, key, smallest, high):
    extent = entries.shape
    index_at = [jax.random.randint(jax.random.fold_in(key, axis), (), 0, extent[axis]) for axis in range(len(extent))]
    entries = entries.at[tuple(index_at)].set(smallest)
    longest = extent.index(max(extent))
    index_at[longest] = (index_at[longest] + 1) % extent[longest]
    return entries.at[tuple(index_at)].set(high)


def block_levels(key, extent, pieces, low, largest):
    gain = 1.0
    for position, blocks in pieces:
        heights = jax.random.uniform(jax.random.fold_in(jax.random.fold_in(key, 6), position), (blocks,), jnp.float32, low / len(pieces), largest / len(pieces))
        gain = gain * jnp.repeat(jnp.exp(heights), extent[position] // blocks).reshape((-1,) + (1,) * (len(extent) - 1 - position))
    return gain


def normal_values(own_key, shape, width, bound, pieces=(), held_as=jnp.bfloat16):
    drawn = jax.random.normal(own_key, shape, jnp.float32) * width
    if len(pieces) > 0:
        drawn = block_levels(own_key, shape, pieces, -0.22, 0.18) * drawn
    return jnp.clip(drawn, min=-bound, max=bound).astype(held_as)


def setup_inputs(seed: int = 0) -> dict:
    splits = jax.random.split(jax.random.key(seed), 7)
    return {
        "snapshots": normal_values(splits[0], (CELLS, TIMES), 1.0, 6.0, ((0, 256),)),
        "range_test": normal_values(splits[1], (TIMES, RANK), TIMES ** -0.5, 0.25),
        "test_rows": normal_values(splits[2], (SKETCH, CELLS), CELLS ** -0.5, 0.00390625, ((1, 256),)),
        "species": set_ends(jax.random.randint(splits[3], (NX, GY), 0, SPECIES), jax.random.fold_in(splits[3], 1), 0, SPECIES - 1).astype(jnp.int32),
        "reaction_rates": jnp.clip(jnp.exp(jax.random.uniform(splits[4], (SPECIES,), jnp.float32, math.log(1.0), math.log(8.0))), 1.0, 8.0),
        "adjoint_end": normal_values(splits[5], (NX, GY), 1.0, 6.0, ((0, 256),), jnp.float32),
    }


DIFFUSION = 0.2
STEP_SIZE = 0.05

def laplace(field):
    padded = jnp.pad(field, 1)
    return padded[2:, 1:-1] + padded[:-2, 1:-1] + padded[1:-1, 2:] + padded[1:-1, :-2] - 4.0 * field

def reference(snapshots, range_test, test_rows, species, reaction_rates, adjoint_end):
    high = lax.Precision.HIGHEST
    range_part = jnp.dot(snapshots.astype(jnp.float32), range_test.astype(jnp.float32), preferred_element_type=jnp.float32)
    gram = jnp.dot(range_part.T, range_part, precision=high)
    lower_factor = jnp.linalg.cholesky(gram)
    basis = jax.scipy.linalg.solve_triangular(lower_factor, range_part.T, lower=True).T
    projected = jnp.dot(test_rows.astype(jnp.float32), basis, precision=high)
    corange = jnp.dot(test_rows.astype(jnp.float32), snapshots.astype(jnp.float32), preferred_element_type=jnp.float32)
    normal_matrix = jnp.dot(projected.T, projected, precision=high)
    normal_factor = jnp.linalg.cholesky(normal_matrix)
    moments = jnp.dot(projected.T, corange, precision=high)
    factors = jax.scipy.linalg.cho_solve((normal_factor, True), moments)
    states = jnp.dot(basis, factors[:, TIMES - 2:], precision=high)
    coupling = reaction_rates[species]
    adjoint = adjoint_end
    for column in (1, 0):
        state = states[:, column].reshape(NX, GY)
        adjoint = adjoint + DIFFUSION * laplace(adjoint) + STEP_SIZE * coupling * (1.0 - 3.0 * state * state) * adjoint
    return (adjoint, factors * CELLS ** (-0.5))
```

```python
import functools

import jax
import jax.numpy as jnp
from jax import lax
from jax.experimental import pallas as pl
from jax.experimental.pallas import tpu as pltpu
from jax.sharding import PartitionSpec as P

DIFFUSION = 0.2
STEP_SIZE = 0.05
MESH = pl.DeviceIdType.MESH
HIGH = lax.Precision.HIGHEST
F32 = jnp.float32
BF16 = jnp.bfloat16

YS, ZS, XS, CS = 4, 8, 4, 2
PLANE = YS * XS * CS
STEPS = 8


def iota(shape, dim):
    return lax.broadcasted_iota(jnp.int32, shape, dim)


def local_kernel(x_ref, psi_ref, om_ref, ar_ref, ct_ref, yt_ref, c_acc, k_acc):
    step = pl.program_id(0)
    x = x_ref[...]
    corange = jnp.dot(psi_ref[...], x, preferred_element_type=F32)
    y = jnp.dot(x, om_ref[...], preferred_element_type=F32)
    yt = y.T
    yt_ref[...] = yt
    hi = y.astype(BF16)
    lo = (y - hi.astype(F32)).astype(BF16)
    hi_t = yt.astype(BF16)
    lo_t = (yt - hi_t.astype(F32)).astype(BF16)
    wide = jnp.concatenate([hi, lo], axis=1)
    wide_t = jnp.concatenate([hi_t, lo_t], axis=0)
    squares = jnp.dot(wide_t, wide, preferred_element_type=F32)

    @pl.when(step == 0)
    def _():
        c_acc[...] = corange
        k_acc[...] = squares

    @pl.when(step > 0)
    def _():
        c_acc[...] += corange
        k_acc[...] += squares

    @pl.when(step == pl.num_programs(0) - 1)
    def _():
        r = RANK = 128
        gram = (
            k_acc[0:r, 0:r] + k_acc[0:r, r : 2 * r] + k_acc[r : 2 * r, 0:r]
            + k_acc[r : 2 * r, r : 2 * r]
        )
        raw = jnp.dot(c_acc[...], om_ref[...].astype(F32), precision=HIGH)
        ar_ref[:, 0:8, :] = raw.reshape(PLANE, 8, RANK)
        row = iota((128, 128), 0)
        source = ((row >> 1) & 7) * 16 + ((row >> 5) & 3) * 4 + ((row >> 4) & 1) * 2 + (row & 1)
        perm = jnp.where(iota((128, 128), 1) == source, 1.0, 0.0).astype(F32)
        for y_at in range(YS):
            block = lax.dot_general(
                perm,
                c_acc[:, y_at * 128 : (y_at + 1) * 128],
                (((1,), (1,)), ((), ())),
                precision=HIGH,
                preferred_element_type=F32,
            )
            ct_ref[8 * y_at : 8 * y_at + 8] = block.reshape(8, 16, 256)
        for k in range(16):
            ar_ref[2 * k, 8:12, :] = gram[8 * k : 8 * k + 4]
            ar_ref[2 * k + 1, 8:12, :] = gram[8 * k + 4 : 8 * k + 8]
        ar_ref[:, 12:16, :] = jnp.zeros((PLANE, 4, 128), F32)
        last = ct_ref[PLANE - 1, 14:16, :]
        ar_ref[0, 12:14, :] = last[:, 0:128]
        ar_ref[0, 14:16, :] = last[:, 128:256]


def local_sums(x, psi, om):
    cells, times = x.shape
    block = cells // STEPS
    sketch, rank = psi.shape[0], om.shape[1]
    return pl.pallas_call(
        local_kernel,
        grid=(STEPS,),
        in_specs=[
            pl.BlockSpec((block, times), lambda i: (i, 0)),
            pl.BlockSpec((sketch, block), lambda i: (0, i)),
            pl.BlockSpec((times, rank), lambda i: (0, 0)),
        ],
        out_specs=[
            pl.BlockSpec((PLANE, 16, 128), lambda i: (0, 0, 0)),
            pl.BlockSpec((PLANE, 16, 256), lambda i: (0, 0, 0)),
            pl.BlockSpec((rank, block), lambda i: (0, i)),
        ],
        out_shape=[
            jax.ShapeDtypeStruct((PLANE, 16, 128), F32),
            jax.ShapeDtypeStruct((PLANE, 16, 256), F32),
            jax.ShapeDtypeStruct((rank, cells), F32),
        ],
        scratch_shapes=[pltpu.VMEM((sketch, times), F32), pltpu.VMEM((256, 256), F32)],
        compiler_params=pltpu.CompilerParams(
            dimension_semantics=("arbitrary",), vmem_limit_bytes=48 << 20
        ),
        name="local_sums",
    )(x, psi, om)


def place():
    s = lax.axis_index("space")
    return s // (ZS * XS), (s // XS) % ZS, s % XS, lax.axis_index("tm")


def plane_peer(q, z):
    return ((q // (XS * CS) * ZS + z) * XS + (q // CS) % XS, q % CS)


def ring_peer(index):
    index = lax.rem(index + 256, 256)
    return (index // CS, index % CS)


def comm_kernel(
    ar, ct, adj, sums, mine, halo,
    ar_in, ct_in, part, z_in, done, ct_part, ctz_in, edge,
    ar_send, ar_recv, ct_send, ct_recv, z_send, z_recv, g_send, g_recv, cz_send, cz_recv,
    h_send, h_recv,
):
    y, z, x, c = place()
    q = (y * XS + x) * CS + c
    me = ((y * ZS + z) * XS + x) * CS + c

    barrier = pltpu.get_barrier_semaphore()

    def greet(d, carry):
        pl.semaphore_signal(
            barrier, inc=1, device_id=plane_peer((q + d) % PLANE, z), device_id_type=MESH
        )
        return carry

    lax.fori_loop(1, PLANE, greet, 0)

    def z_peer(zz):
        return ((y * ZS + zz) * XS + x, c)

    for d in range(1, ZS):
        pl.semaphore_signal(barrier, inc=1, device_id=z_peer((z + d) % ZS), device_id_type=MESH)
    for d in (1, -1):
        pl.semaphore_signal(barrier, inc=1, device_id=ring_peer(me + d), device_id_type=MESH)
    pl.semaphore_wait(barrier, PLANE - 1 + ZS - 1 + 2)

    def ar_copy(to, slot_from, slot_to, send):
        return pltpu.make_async_remote_copy(
            src_ref=ar.at[slot_from], dst_ref=ar_in.at[slot_to],
            send_sem=ar_send.at[send], recv_sem=ar_recv.at[slot_to],
            device_id=to, device_id_type=MESH,
        )

    def ct_copy(to, slot_from, slot_to, send):
        return pltpu.make_async_remote_copy(
            src_ref=ct.at[slot_from], dst_ref=ct_in.at[slot_to],
            send_sem=ct_send.at[send], recv_sem=ct_recv.at[slot_to],
            device_id=to, device_id_type=MESH,
        )

    def z_copy(to, slot_to, send):
        return pltpu.make_async_remote_copy(
            src_ref=part, dst_ref=z_in.at[slot_to],
            send_sem=z_send.at[send], recv_sem=z_recv.at[slot_to],
            device_id=to, device_id_type=MESH,
        )

    def g_copy(to, slot_to, send):
        return pltpu.make_async_remote_copy(
            src_ref=done, dst_ref=sums.at[slot_to],
            send_sem=g_send.at[send], recv_sem=g_recv.at[slot_to],
            device_id=to, device_id_type=MESH,
        )

    def cz_copy(to, slot_from, slot_to, send):
        return pltpu.make_async_remote_copy(
            src_ref=ct_part.at[slot_from], dst_ref=ctz_in.at[slot_to],
            send_sem=cz_send.at[send], recv_sem=cz_recv.at[slot_to],
            device_id=to, device_id_type=MESH,
        )

    def h_copy(which):
        return pltpu.make_async_remote_copy(
            src_ref=edge.at[which], dst_ref=halo.at[which],
            send_sem=h_send.at[which], recv_sem=h_recv.at[which],
            device_id=ring_peer(me + (1 if which == 0 else -1)), device_id_type=MESH,
        )

    edge[0] = adj[7:8, :]
    edge[1] = adj[0:1, :]

    def loop(low, high, body):
        def step(d, carry):
            body(d)
            return carry

        lax.fori_loop(low, high, step, 0)

    loop(1, PLANE, lambda d: ar_copy(
        plane_peer((q + d) % PLANE, z), (q + d) % PLANE, q, d).start())
    loop(1, PLANE, lambda d: ct_copy(
        plane_peer((q + d) % PLANE, z), (q + d) % PLANE, q, d).start())
    h_copy(0).start()
    h_copy(1).start()
    ar_in[q] = ar[q]
    ct_in[q] = ct[q]
    loop(1, PLANE, lambda d: ar_copy(
        plane_peer((q + d) % PLANE, z), q, (q + d) % PLANE, d).wait_recv())
    part[...] = jnp.sum(ar_in[...], axis=0)

    for d in range(1, ZS):
        z_copy(z_peer((z + d) % ZS), z, d).start()
    z_in[z] = part[...]
    for d in range(1, ZS):
        z_copy(z_peer((z + d) % ZS), (z + d) % ZS, d).wait_recv()
    total = jnp.sum(z_in[...], axis=0)
    done[...] = total

    loop(1, PLANE, lambda d: g_copy(plane_peer((q + d) % PLANE, z), q, d).start())
    sums[q] = total

    loop(1, PLANE, lambda d: ct_copy(
        plane_peer((q + d) % PLANE, z), q, (q + d) % PLANE, d).wait_recv())
    ct_sum = jnp.sum(ct_in[...], axis=0)
    for zz in range(ZS):
        ct_part[zz] = ct_sum[2 * zz : 2 * zz + 2]
    for d in range(1, ZS):
        cz_copy(z_peer((z + d) % ZS), (z + d) % ZS, z, d).start()
    ctz_in[z] = ct_part[z]

    loop(1, PLANE, lambda d: g_copy(
        plane_peer((q + d) % PLANE, z), (q + d) % PLANE, d).wait_recv())
    for d in range(1, ZS):
        cz_copy(z_peer((z + d) % ZS), z, (z + d) % ZS, d).wait_recv()
    mine[...] = jnp.sum(ctz_in[...], axis=0)

    h_copy(0).wait_recv()
    h_copy(1).wait_recv()
    h_copy(0).wait_send()
    h_copy(1).wait_send()
    loop(1, PLANE, lambda d: ar_copy(plane_peer(q, z), q, q, d).wait_send())
    loop(1, PLANE, lambda d: ct_copy(plane_peer(q, z), q, q, d).wait_send())
    loop(1, PLANE, lambda d: g_copy(plane_peer(q, z), q, d).wait_send())
    for d in range(1, ZS):
        z_copy(z_peer(z), z, d).wait_send()
        cz_copy(z_peer(z), z, z, d).wait_send()


def exchange(ar, ct, adj):
    vmem = pl.BlockSpec(memory_space=pltpu.VMEM)
    dma = pltpu.SemaphoreType.DMA
    width = adj.shape[1]
    return pl.pallas_call(
        comm_kernel,
        in_specs=[vmem] * 3,
        out_specs=[vmem] * 3,
        out_shape=[
            jax.ShapeDtypeStruct((PLANE, 16, 128), F32),
            jax.ShapeDtypeStruct((2, 256), F32),
            jax.ShapeDtypeStruct((2, 1, width), F32),
        ],
        scratch_shapes=[
            pltpu.VMEM((PLANE, 16, 128), F32),
            pltpu.VMEM((PLANE, 16, 256), F32),
            pltpu.VMEM((16, 128), F32),
            pltpu.VMEM((ZS, 16, 128), F32),
            pltpu.VMEM((16, 128), F32),
            pltpu.VMEM((ZS, 2, 256), F32),
            pltpu.VMEM((ZS, 2, 256), F32),
            pltpu.VMEM((2, 1, width), F32),
            dma((PLANE,)), dma((PLANE,)), dma((PLANE,)), dma((PLANE,)),
            dma((ZS,)), dma((ZS,)), dma((PLANE,)), dma((PLANE,)),
            dma((ZS,)), dma((ZS,)), dma((2,)), dma((2,)),
        ],
        compiler_params=pltpu.CompilerParams(collective_id=0, has_side_effects=True),
        name="exchange",
    )(ar, ct, adj)


def lane(a, k):
    return jnp.broadcast_to(a[:, k : k + 1], (8, 128))


def sub(a, k):
    return jnp.broadcast_to(a[k : k + 1, :], (8, 128))


def panel_steps(panel, k0, in_place):
    subs, lanes = iota((8, 128), 0), iota((8, 128), 1)
    cols = [lane(panel, k0 + j) for j in range(8)]
    upper = jnp.zeros((8, 128), F32)
    for i in range(8):
        here = subs == i
        pivot = sub(cols[i], i)
        inverse = 1.0 / pivot
        if in_place:
            panel = jnp.where(lanes == k0 + i, jnp.where(here, 1.0, 0.0), panel)
        else:
            upper = jnp.where(here & (lanes >= k0 + i), panel * lax.rsqrt(pivot), upper)
        row = sub(panel, i) * inverse
        panel = jnp.where(here, row, panel - cols[i] * row)
        for j in range(i + 1, 8):
            entry = sub(cols[j], i) * inverse
            cols[j] = jnp.where(here, entry, cols[j] - cols[i] * entry)
    return panel, upper


def upper_factor(rows):
    rows = list(rows)
    out = []
    for k in range(16):
        k0 = 8 * k
        panel, upper = panel_steps(rows[k], k0, False)
        out.append(upper)
        pieces = [sub(panel, j) for j in range(8)]
        for b in range(k + 1, 16):
            update = lane(rows[b], k0) * pieces[0]
            for j in range(1, 8):
                update = update + lane(rows[b], k0 + j) * pieces[j]
            rows[b] = rows[b] - update
    return out


def solve_rows(rows, right):
    rows = list(rows)
    lanes = iota((8, 128), 1)
    for k in range(16):
        k0 = 8 * k
        inside = (lanes >= k0) & (lanes < k0 + 8)
        panel, _ = panel_steps(rows[k], k0, True)
        panel = jnp.where(inside, -panel, panel)
        pieces = [sub(panel, j) for j in range(8)]
        for b in range(k + 1, 17):
            old = right if b == 16 else rows[b]
            update = lane(old, k0) * pieces[0]
            for j in range(1, 8):
                update = update + lane(old, k0 + j) * pieces[j]
            new = jnp.where(inside, 0.0, old) - update
            if b == 16:
                right = new
            else:
                rows[b] = new
    return right


def shifted(field, low, high):
    up = jnp.concatenate([low, field[0:7]], axis=0)
    down = jnp.concatenate([field[1:8], high], axis=0)
    nothing = jnp.zeros((8, 1), F32)
    left = jnp.concatenate([nothing, field[:, :-1]], axis=1)
    right = jnp.concatenate([field[:, 1:], nothing], axis=1)
    return up + down + left + right - 4.0 * field


def masked_halo(halo, me):
    low = jnp.where(me == 0, 0.0, halo[0])
    high = jnp.where(me == 255, 0.0, halo[1])
    return low, high


def solve_kernel(
    sums, mine, halo, yt_hbm, adj, species, rates, me_ref, adj_out, growth_out, t_out, yt, sem
):
    fetch = pltpu.make_async_copy(yt_hbm, yt, sem)
    fetch.start()
    raw = sums[:, 0:8, :].reshape(256, 128)
    gram = [
        jnp.concatenate([sums[2 * k, 8:12, :], sums[2 * k + 1, 8:12, :]], axis=0)
        for k in range(16)
    ]
    last = jnp.concatenate([sums[0, 12:14, :], sums[0, 14:16, :]], axis=1)
    right = jnp.concatenate([mine[...], last, jnp.zeros((4, 256), F32)], axis=0)
    right = jnp.dot(right, raw, precision=HIGH)
    normal = lax.dot_general(raw, raw, (((0,), (0,)), ((), ())), precision=HIGH)
    upper = upper_factor(gram)
    solved = solve_rows([normal[8 * k : 8 * k + 8] for k in range(16)], right)
    factor = jnp.concatenate(upper, axis=0)
    t_out[...] = lax.dot_general(
        solved, factor, (((1,), (1,)), ((), ())), precision=HIGH
    ) * (2097152.0 ** -0.5)
    columns = jnp.concatenate([solved] * 16, axis=0).T

    kinds = species[...]
    coupling = jnp.zeros(kinds.shape, F32)
    for kind in range(4):
        coupling = jnp.where(kinds == kind, rates[kind], coupling)

    fetch.wait()

    def state(j):
        weights = jnp.broadcast_to(columns[:, j : j + 1], (128, 128))
        tiles = []
        for b in range(8):
            parts = []
            for xx in range(8):
                at = xx * 1024 + b * 128
                parts.append(jnp.sum(yt[:, at : at + 128] * weights, axis=0, keepdims=True))
            tiles.append(jnp.concatenate(parts, axis=0))
        return jnp.concatenate(tiles, axis=1)

    first, second = state(3), state(2)
    field = adj[...]
    low, high = masked_halo(halo, me_ref[0])
    adj_out[...] = (
        field
        + DIFFUSION * shifted(field, low, high)
        + STEP_SIZE * coupling * (1.0 - 3.0 * first * first) * field
    )
    growth_out[...] = STEP_SIZE * coupling * (1.0 - 3.0 * second * second)


def solve(sums, mine, halo, yt, adj, species, rates, me):
    vmem = pl.BlockSpec(memory_space=pltpu.VMEM)
    smem = pl.BlockSpec(memory_space=pltpu.SMEM)
    return pl.pallas_call(
        solve_kernel,
        in_specs=[vmem, vmem, vmem, pl.BlockSpec(memory_space=pl.ANY), vmem, vmem, smem, smem],
        out_specs=[vmem] * 3,
        out_shape=[
            jax.ShapeDtypeStruct(adj.shape, F32),
            jax.ShapeDtypeStruct(adj.shape, F32),
            jax.ShapeDtypeStruct((8, 128), F32),
        ],
        scratch_shapes=[pltpu.VMEM(yt.shape, F32), pltpu.SemaphoreType.DMA],
        compiler_params=pltpu.CompilerParams(vmem_limit_bytes=48 << 20),
        name="solve",
    )(sums, mine, halo, yt, adj, species, rates, me)


def last_kernel(adj, growth, out, edge, halo, send, recv):
    y, z, x, c = place()
    me = ((y * ZS + z) * XS + x) * CS + c
    barrier = pltpu.get_barrier_semaphore()
    for d in (1, -1):
        pl.semaphore_signal(barrier, inc=1, device_id=ring_peer(me + d), device_id_type=MESH)
    edge[0] = adj[7:8, :]
    edge[1] = adj[0:1, :]
    pl.semaphore_wait(barrier, 2)

    def copy(which):
        return pltpu.make_async_remote_copy(
            src_ref=edge.at[which], dst_ref=halo.at[which],
            send_sem=send.at[which], recv_sem=recv.at[which],
            device_id=ring_peer(me + (1 if which == 0 else -1)), device_id_type=MESH,
        )

    copy(0).start()
    copy(1).start()
    field = adj[...]
    copy(0).wait()
    copy(1).wait()
    low, high = masked_halo(halo, me)
    out[...] = field + DIFFUSION * shifted(field, low, high) + growth[...] * field


def last_step(adj, growth):
    vmem = pl.BlockSpec(memory_space=pltpu.VMEM)
    dma = pltpu.SemaphoreType.DMA
    return pl.pallas_call(
        last_kernel,
        in_specs=[vmem] * 2,
        out_specs=vmem,
        out_shape=jax.ShapeDtypeStruct(adj.shape, F32),
        scratch_shapes=[
            pltpu.VMEM((2, 1, adj.shape[1]), F32),
            pltpu.VMEM((2, 1, adj.shape[1]), F32),
            dma((2,)), dma((2,)),
        ],
        compiler_params=pltpu.CompilerParams(collective_id=1, has_side_effects=True),
        name="last_step",
    )(adj, growth)


def shards(snapshots, range_test, test_rows, species, reaction_rates, adjoint_end):
    ar, ct, yt = local_sums(snapshots, test_rows, range_test)
    sums, mine, halo = exchange(ar, ct, adjoint_end)
    me = (lax.axis_index("space") * CS + lax.axis_index("tm")).astype(jnp.int32).reshape(1)
    adjoint, growth, factors = solve(
        sums, mine, halo, yt, adjoint_end, species, reaction_rates, me
    )
    adjoint = last_step(adjoint, growth)
    return adjoint, factors[0:2].T


def solution(mesh):
    cells = ("space", "tm")
    in_specs = (P(cells, None), P(), P(None, cells), P(cells, None), P(), P(cells, None))
    out_specs = (P(cells, None), P(None, cells))
    return jax.shard_map(
        shards, mesh=mesh, in_specs=in_specs, out_specs=out_specs, check_vma=False
    )
```

```python
import functools

import jax
import jax.numpy as jnp
from jax import lax
from jax.experimental import pallas as pl
from jax.experimental.pallas import tpu as pltpu
from jax.sharding import PartitionSpec as P

DIFFUSION = 0.2
STEP_SIZE = 0.05
MESH = pl.DeviceIdType.MESH
HIGH = lax.Precision.HIGHEST
F32 = jnp.float32
BF16 = jnp.bfloat16

YS, ZS, XS, CS = 4, 8, 4, 2
PLANE = YS * XS * CS
STEPS = 8
WIDTH = 1024


def iota(shape, dim):
    return lax.broadcasted_iota(jnp.int32, shape, dim)


def place():
    s = lax.axis_index("space")
    return s // (ZS * XS), (s // XS) % ZS, s % XS, lax.axis_index("tm")


def plane_peer(q, z):
    return ((q // (XS * CS) * ZS + z) * XS + (q // CS) % XS, q % CS)


def ring_peer(index):
    index = lax.rem(index + 256, 256)
    return (index // CS, index % CS)


def lane(a, k):
    return jnp.broadcast_to(a[:, k : k + 1], (8, 128))


def sub(a, k):
    return jnp.broadcast_to(a[k : k + 1, :], (8, 128))


def panel_steps(panel, k0, in_place):
    subs, lanes = iota((8, 128), 0), iota((8, 128), 1)
    cols = [lane(panel, k0 + j) for j in range(8)]
    upper = jnp.zeros((8, 128), F32)
    for i in range(8):
        here = subs == i
        pivot = sub(cols[i], i)
        inverse = 1.0 / pivot
        if in_place:
            panel = jnp.where(lanes == k0 + i, jnp.where(here, 1.0, 0.0), panel)
        else:
            upper = jnp.where(here & (lanes >= k0 + i), panel * lax.rsqrt(pivot), upper)
        row = sub(panel, i) * inverse
        panel = jnp.where(here, row, panel - cols[i] * row)
        for j in range(i + 1, 8):
            entry = sub(cols[j], i) * inverse
            cols[j] = jnp.where(here, entry, cols[j] - cols[i] * entry)
    return panel, upper


def upper_factor(rows):
    rows = list(rows)
    out = []
    for k in range(16):
        k0 = 8 * k
        panel, upper = panel_steps(rows[k], k0, False)
        out.append(upper)
        pieces = [sub(panel, j) for j in range(8)]
        for b in range(k + 1, 16):
            update = lane(rows[b], k0) * pieces[0]
            for j in range(1, 8):
                update = update + lane(rows[b], k0 + j) * pieces[j]
            rows[b] = rows[b] - update
    return out


def solve_rows(rows, right):
    rows = list(rows)
    lanes = iota((8, 128), 1)
    for k in range(16):
        k0 = 8 * k
        inside = (lanes >= k0) & (lanes < k0 + 8)
        panel, _ = panel_steps(rows[k], k0, True)
        panel = jnp.where(inside, -panel, panel)
        pieces = [sub(panel, j) for j in range(8)]
        for b in range(k + 1, 17):
            old = right if b == 16 else rows[b]
            update = lane(old, k0) * pieces[0]
            for j in range(1, 8):
                update = update + lane(old, k0 + j) * pieces[j]
            new = jnp.where(inside, 0.0, old) - update
            if b == 16:
                right = new
            else:
                rows[b] = new
    return right


def sideways(field):
    nothing = jnp.zeros((field.shape[0], 1), F32)
    left = jnp.concatenate([nothing, field[:, :-1]], axis=1)
    right = jnp.concatenate([field[:, 1:], nothing], axis=1)
    return left + right - 4.0 * field


def coupling_of(kinds, rates):
    coupling = jnp.zeros(kinds.shape, F32)
    for kind in range(4):
        coupling = jnp.where(kinds == kind, rates[kind], coupling)
    return coupling


def loop(low, high, body):
    def step(d, carry):
        body(d)
        return carry

    lax.fori_loop(low, high, step, 0)


def whole_kernel(
    x_hbm, om_hbm, psi_hbm, spec_hbm, rates, adj_hbm,
    adj_out, t_out,
    xb, psib, omb, spec, adj, yt, c_acc, k_acc,
    ar, ct, ar_in, ct_in, part, z_in, done, sums, ct_part, ctz_in, edge, halo, halo_y,
    x_sem, psi_sem, small_sem,
    ar_send, ar_recv, ct_send, ct_recv, z_send, z_recv, g_send, g_recv, cz_send, cz_recv,
    h_send, h_recv, y_send, y_recv,
):
    y, z, x, c = place()
    q = (y * XS + x) * CS + c
    me = ((y * ZS + z) * XS + x) * CS + c

    def x_copy(k):
        return pltpu.make_async_copy(
            x_hbm.at[pl.ds(k * WIDTH, WIDTH), :], xb.at[k], x_sem.at[k])

    def psi_copy(k):
        return pltpu.make_async_copy(
            psi_hbm.at[:, pl.ds(k * WIDTH, WIDTH)], psib.at[k], psi_sem.at[k])

    om_copy = pltpu.make_async_copy(om_hbm, omb, small_sem.at[0])
    spec_copy = pltpu.make_async_copy(spec_hbm, spec, small_sem.at[1])
    adj_copy = pltpu.make_async_copy(adj_hbm, adj, small_sem.at[2])
    om_copy.start()
    for i in range(STEPS):
        x_copy((i + 7) % STEPS).start()
        psi_copy((i + 7) % STEPS).start()
        if i == 1:
            spec_copy.start()
            adj_copy.start()

    barrier = pltpu.get_barrier_semaphore()
    loop(1, PLANE, lambda d: pl.semaphore_signal(
        barrier, inc=1, device_id=plane_peer((q + d) % PLANE, z), device_id_type=MESH))

    def z_peer(zz):
        return ((y * ZS + zz) * XS + x, c)

    for d in range(1, ZS):
        pl.semaphore_signal(barrier, inc=1, device_id=z_peer((z + d) % ZS), device_id_type=MESH)
    for d in (1, -1):
        pl.semaphore_signal(barrier, inc=1, device_id=ring_peer(me + d), device_id_type=MESH)

    def ar_copy(to, slot_from, slot_to, send):
        return pltpu.make_async_remote_copy(
            src_ref=ar.at[slot_from], dst_ref=ar_in.at[slot_to],
            send_sem=ar_send.at[send], recv_sem=ar_recv.at[slot_to],
            device_id=to, device_id_type=MESH)

    def ct_copy(to, slot_from, slot_to, send):
        return pltpu.make_async_remote_copy(
            src_ref=ct.at[slot_from], dst_ref=ct_in.at[slot_to],
            send_sem=ct_send.at[send], recv_sem=ct_recv.at[slot_to],
            device_id=to, device_id_type=MESH)

    def z_copy(to, slot_to, send):
        return pltpu.make_async_remote_copy(
            src_ref=part, dst_ref=z_in.at[slot_to],
            send_sem=z_send.at[send], recv_sem=z_recv.at[slot_to],
            device_id=to, device_id_type=MESH)

    def g_copy(to, slot_to, send):
        return pltpu.make_async_remote_copy(
            src_ref=done, dst_ref=sums.at[slot_to],
            send_sem=g_send.at[send], recv_sem=g_recv.at[slot_to],
            device_id=to, device_id_type=MESH)

    def cz_copy(to, slot_from, slot_to, send):
        return pltpu.make_async_remote_copy(
            src_ref=ct_part.at[slot_from], dst_ref=ctz_in.at[slot_to],
            send_sem=cz_send.at[send], recv_sem=cz_recv.at[slot_to],
            device_id=to, device_id_type=MESH)

    def h_copy(which):
        return pltpu.make_async_remote_copy(
            src_ref=edge.at[which], dst_ref=halo.at[which],
            send_sem=h_send.at[which], recv_sem=h_recv.at[which],
            device_id=ring_peer(me + (1 if which == 0 else -1)), device_id_type=MESH)

    def y_copy(which):
        return pltpu.make_async_remote_copy(
            src_ref=yt.at[7 if which == 0 else 0], dst_ref=halo_y.at[which],
            send_sem=y_send.at[which], recv_sem=y_recv.at[which],
            device_id=ring_peer(me + (1 if which == 0 else -1)), device_id_type=MESH)

    om_copy.wait()
    c_acc[...] = jnp.zeros_like(c_acc)
    k_acc[...] = jnp.zeros_like(k_acc)

    def block(i):
        k = (i + 7) % STEPS
        x_copy(k).wait()
        psi_copy(k).wait()
        xs = xb[k]
        ys = jnp.dot(xs, omb[...], preferred_element_type=F32)
        ys_t = ys.T
        yt[k] = ys_t
        hi = ys.astype(BF16)
        lo = (ys - hi.astype(F32)).astype(BF16)
        hi_t = ys_t.astype(BF16)
        lo_t = (ys_t - hi_t.astype(F32)).astype(BF16)
        wide = jnp.concatenate([hi, lo], axis=1)
        wide_t = jnp.concatenate([hi_t, lo_t], axis=0)
        k_acc[...] += jnp.dot(wide_t, wide, preferred_element_type=F32)
        c_acc[...] += jnp.dot(psib[k], xs, preferred_element_type=F32)

    loop(0, 2, block)
    spec_copy.wait()
    adj_copy.wait()
    coupling = coupling_of(spec[...], rates)
    edge[0, 0:1] = adj[7:8, :]
    edge[0, 1:2] = adj[6:7, :]
    edge[0, 2:3] = coupling[7:8, :]
    edge[0, 3:4] = coupling[7:8, :]
    edge[1, 0:1] = adj[0:1, :]
    edge[1, 1:2] = adj[1:2, :]
    edge[1, 2:3] = coupling[0:1, :]
    edge[1, 3:4] = coupling[0:1, :]
    pl.semaphore_wait(barrier, PLANE - 1 + ZS - 1 + 2)
    for which in range(2):
        y_copy(which).start()
        h_copy(which).start()
    loop(2, STEPS, block)

    r = 128
    gram = k_acc[0:r, 0:r] + k_acc[0:r, r:] + k_acc[r:, 0:r] + k_acc[r:, r:]
    om_f = omb[...]
    c_all = c_acc[...]
    c_1 = c_all.astype(BF16)
    rest = c_all - c_1.astype(F32)
    c_2 = rest.astype(BF16)
    c_3 = (rest - c_2.astype(F32)).astype(BF16)
    raw = (
        jnp.dot(c_3, om_f, preferred_element_type=F32)
        + jnp.dot(c_2, om_f, preferred_element_type=F32)
        + jnp.dot(c_1, om_f, preferred_element_type=F32)
    )
    ar[:, 0:8, :] = raw.reshape(PLANE, 8, r)
    for k in range(16):
        ar[2 * k, 8:12, :] = gram[8 * k : 8 * k + 4]
        ar[2 * k + 1, 8:12, :] = gram[8 * k + 4 : 8 * k + 8]
    row = iota((r, r), 0)
    source = ((row >> 1) & 7) * 16 + ((row >> 5) & 3) * 4 + ((row >> 4) & 1) * 2 + (row & 1)
    perm = jnp.where(iota((r, r), 1) == source, 1.0, 0.0).astype(F32)

    def turned(y_at):
        piece = lax.dot_general(
            perm, c_acc[:, y_at * r : (y_at + 1) * r], (((1,), (1,)), ((), ())),
            precision=HIGH, preferred_element_type=F32)
        ct[8 * y_at : 8 * y_at + 8] = piece.reshape(8, 16, 256)

    turned(YS - 1)
    ar[:, 12:16, :] = jnp.zeros((PLANE, 4, r), F32)
    ends = ct[PLANE - 1, 14:16, :]
    ar[0, 12:14, :] = ends[:, 0:128]
    ar[0, 14:16, :] = ends[:, 128:256]

    loop(1, PLANE, lambda d: ar_copy(
        plane_peer((q + d) % PLANE, z), (q + d) % PLANE, q, d).start())
    ar_in[q] = ar[q]
    for y_at in range(YS - 1):
        turned(y_at)
    ct_in[q] = ct[q]
    loop(1, PLANE, lambda d: ar_copy(
        plane_peer((q + d) % PLANE, z), q, (q + d) % PLANE, d).wait_recv())
    part[...] = jnp.sum(ar_in[...], axis=0)

    for d in range(1, ZS):
        z_copy(z_peer((z + d) % ZS), z, d).start()
    loop(1, PLANE, lambda d: ct_copy(
        plane_peer((q + d) % PLANE, z), (q + d) % PLANE, q, d).start())
    z_in[z] = part[...]
    for d in range(1, ZS):
        z_copy(z_peer((z + d) % ZS), (z + d) % ZS, d).wait_recv()
    total = jnp.sum(z_in[...], axis=0)
    done[...] = total

    loop(1, PLANE, lambda d: g_copy(plane_peer((q + d) % PLANE, z), q, d).start())
    sums[q] = total

    loop(1, PLANE, lambda d: ct_copy(
        plane_peer((q + d) % PLANE, z), q, (q + d) % PLANE, d).wait_recv())
    ct_sum = jnp.sum(ct_in[...], axis=0)
    for zz in range(ZS):
        ct_part[zz] = ct_sum[2 * zz : 2 * zz + 2]
    for d in range(1, ZS):
        cz_copy(z_peer((z + d) % ZS), (z + d) % ZS, z, d).start()
    ctz_in[z] = ct_part[z]

    loop(1, PLANE, lambda d: g_copy(
        plane_peer((q + d) % PLANE, z), (q + d) % PLANE, d).wait_recv())
    for d in range(1, ZS):
        cz_copy(z_peer((z + d) % ZS), z, (z + d) % ZS, d).wait_recv()
    mine = jnp.sum(ctz_in[...], axis=0)

    raw = sums[:, 0:8, :].reshape(256, r)
    gram_rows = [
        jnp.concatenate([sums[2 * k, 8:12, :], sums[2 * k + 1, 8:12, :]], axis=0)
        for k in range(16)
    ]
    last = jnp.concatenate([sums[0, 12:14, :], sums[0, 14:16, :]], axis=1)
    right = jnp.concatenate([mine, last, jnp.zeros((4, 256), F32)], axis=0)
    right = jnp.dot(right, raw, precision=HIGH)
    normal = lax.dot_general(raw, raw, (((0,), (0,)), ((), ())), precision=HIGH)
    upper = upper_factor(gram_rows)
    solved = solve_rows([normal[8 * k : 8 * k + 8] for k in range(16)], right)
    factor = jnp.concatenate(upper, axis=0)
    times = lax.dot_general(
        solved, factor, (((1,), (1,)), ((), ())), precision=HIGH
    ) * (2097152.0 ** -0.5)
    t_out[...] = times[0:2]
    columns = jnp.concatenate([solved] * 16, axis=0).T

    def state(blocks, j):
        weights = jnp.broadcast_to(columns[:, j : j + 1], (r, r))
        tiles = []
        for b in range(8):
            tiles.append(jnp.concatenate([
                jnp.sum(get(b * r) * weights, axis=0, keepdims=True) for get in blocks
            ], axis=0))
        return jnp.concatenate(tiles, axis=1)

    own = [functools.partial(lambda k, at: yt[k, :, at : at + r], k) for k in range(8)]
    y_copy(0).wait_recv()
    y_copy(1).wait_recv()
    h_copy(0).wait_recv()
    h_copy(1).wait_recv()
    outer = [functools.partial(lambda k, at: halo_y[k, :, at : at + r], k) for k in range(2)]
    first, second, edges = state(own, 3), state(own, 2), state(outer, 3)

    coupling = STEP_SIZE * coupling_of(spec[...], rates)
    field = adj[...]
    near = jnp.concatenate([halo[0, 0:1], halo[1, 0:1]], axis=0)
    far = jnp.concatenate([halo[0, 1:2], halo[1, 1:2]], axis=0)
    rate = jnp.concatenate([halo[0, 2:3], halo[1, 2:3]], axis=0) * STEP_SIZE
    inner = jnp.concatenate([field[0:1], field[7:8]], axis=0)
    side = iota((2, WIDTH), 0)
    absent = ((side == 0) & (me == 0)) | ((side == 1) & (me == 255))
    near = jnp.where(absent, 0.0, near)
    near_next = (
        near + DIFFUSION * (far + inner + sideways(near))
        + rate * (1.0 - 3.0 * edges * edges) * near
    )
    near_next = jnp.where(absent, 0.0, near_next)

    def advance(field, low, high, state):
        up = jnp.concatenate([low, field[0:7]], axis=0)
        down = jnp.concatenate([field[1:8], high], axis=0)
        return (
            field + DIFFUSION * (up + down + sideways(field))
            + coupling * (1.0 - 3.0 * state * state) * field
        )

    field = advance(field, near[0:1], near[1:2], first)
    adj_out[...] = advance(field, near_next[0:1], near_next[1:2], second)

    for which in range(2):
        h_copy(which).wait_send()
        y_copy(which).wait_send()
    loop(1, PLANE, lambda d: ar_copy(plane_peer(q, z), q, q, d).wait_send())
    loop(1, PLANE, lambda d: ct_copy(plane_peer(q, z), q, q, d).wait_send())
    loop(1, PLANE, lambda d: g_copy(plane_peer(q, z), q, d).wait_send())
    for d in range(1, ZS):
        z_copy(z_peer(z), z, d).wait_send()
        cz_copy(z_peer(z), z, z, d).wait_send()


def shards(snapshots, range_test, test_rows, species, reaction_rates, adjoint_end):
    vmem = pl.BlockSpec(memory_space=pltpu.VMEM)
    smem = pl.BlockSpec(memory_space=pltpu.SMEM)
    hbm = pl.BlockSpec(memory_space=pl.ANY)
    dma = pltpu.SemaphoreType.DMA
    buffer = pltpu.VMEM
    adjoint, factors = pl.pallas_call(
        whole_kernel,
        in_specs=[hbm, hbm, hbm, hbm, smem, hbm],
        out_specs=[vmem] * 2,
        out_shape=[
            jax.ShapeDtypeStruct((8, WIDTH), F32),
            jax.ShapeDtypeStruct((2, 128), F32),
        ],
        scratch_shapes=[
            buffer((STEPS, WIDTH, 512), BF16),
            buffer((STEPS, 256, WIDTH), BF16),
            buffer((512, 128), BF16),
            buffer((8, WIDTH), jnp.int32),
            buffer((8, WIDTH), F32),
            buffer((STEPS, 128, WIDTH), F32),
            buffer((256, 512), F32),
            buffer((256, 256), F32),
            buffer((PLANE, 16, 128), F32),
            buffer((PLANE, 16, 256), F32),
            buffer((PLANE, 16, 128), F32),
            buffer((PLANE, 16, 256), F32),
            buffer((16, 128), F32),
            buffer((ZS, 16, 128), F32),
            buffer((16, 128), F32),
            buffer((PLANE, 16, 128), F32),
            buffer((ZS, 2, 256), F32),
            buffer((ZS, 2, 256), F32),
            buffer((2, 4, WIDTH), F32),
            buffer((2, 4, WIDTH), F32),
            buffer((2, 128, WIDTH), F32),
            dma((STEPS,)), dma((STEPS,)), dma((3,)),
            dma((PLANE,)), dma((PLANE,)), dma((PLANE,)), dma((PLANE,)),
            dma((ZS,)), dma((ZS,)), dma((PLANE,)), dma((PLANE,)),
            dma((ZS,)), dma((ZS,)), dma((2,)), dma((2,)), dma((2,)), dma((2,)),
        ],
        compiler_params=pltpu.CompilerParams(
            collective_id=0, has_side_effects=True, vmem_limit_bytes=56 << 20
        ),
        name="whole",
    )(snapshots, range_test, test_rows, species, reaction_rates, adjoint_end)
    return adjoint, factors.T


def solution(mesh):
    cells = ("space", "tm")
    in_specs = (P(cells, None), P(), P(None, cells), P(cells, None), P(), P(cells, None))
    out_specs = (P(cells, None), P(None, cells))
    return jax.shard_map(
        shards, mesh=mesh, in_specs=in_specs, out_specs=out_specs, check_vma=False
    )
```

```python
import functools

import jax
import jax.numpy as jnp
from jax import lax
from jax.experimental import pallas as pl
from jax.experimental.pallas import tpu as pltpu
from jax.sharding import PartitionSpec as P

DIFFUSION = 0.2
STEP_SIZE = 0.05
MESH = pl.DeviceIdType.MESH
HIGH = lax.Precision.HIGHEST
F32 = jnp.float32
BF16 = jnp.bfloat16

YS, ZS, XS, CS = 4, 8, 4, 2
PLANE = YS * XS * CS
STEPS = 8
WIDTH = 1024
AHEAD = 4


def iota(shape, dim):
    return lax.broadcasted_iota(jnp.int32, shape, dim)


def place():
    s = lax.axis_index("space")
    return (
        lax.div(s, ZS * XS), lax.rem(lax.div(s, XS), ZS), lax.rem(s, XS), lax.axis_index("tm")
    )


def lane(a, k):
    return jnp.broadcast_to(a[:, k : k + 1], (8, 128))


def sub(a, k):
    return jnp.broadcast_to(a[k : k + 1, :], (8, 128))


def product(old, k0, pieces):
    terms = [lane(old, k0 + j) * pieces[j] for j in range(8)]
    while len(terms) > 1:
        terms = [terms[i] + terms[i + 1] for i in range(0, len(terms), 2)]
    return terms[0]


def panel_steps(panel, k0, in_place, zero):
    subs, lanes = iota((8, 128), 0), iota((8, 128), 1)
    cols = [lane(panel, k0 + j) + zero for j in range(8)]
    upper = jnp.zeros((8, 128), F32)
    for i in range(8):
        here = subs == i
        pivot = sub(cols[i], i)
        inverse = 1.0 / pivot
        if in_place:
            panel = jnp.where(lanes == k0 + i, jnp.where(here, 1.0, 0.0), panel)
        else:
            upper = jnp.where(here & (lanes >= k0 + i), panel * lax.rsqrt(pivot), upper)
        row = sub(panel, i) * inverse
        panel = jnp.where(here, row, panel - cols[i] * row)
        for j in range(i + 1, 8):
            entry = sub(cols[j], i) * inverse
            cols[j] = jnp.where(here, entry, cols[j] - cols[i] * entry)
        yield
    return panel, upper


def upper_factor(rows, zero, out):
    rows = list(rows)
    for k in range(16):
        k0 = 8 * k
        panel, upper = yield from panel_steps(rows[k], k0, False, zero)
        out.append(upper)
        pieces = [sub(panel, j) for j in range(8)]
        for b in range(k + 1, 16):
            rows[b] = rows[b] - product(rows[b], k0, pieces)
            yield


def solve_rows(rows, right, zero, out):
    rows = list(rows) + [right]
    lanes = iota((8, 128), 1)
    for k in range(16):
        k0 = 8 * k
        inside = (lanes >= k0) & (lanes < k0 + 8)
        panel, _ = yield from panel_steps(rows[k], k0, True, zero)
        panel = jnp.where(inside, -panel, panel)
        pieces = [sub(panel, j) for j in range(8)]
        for b in range(k + 1, 17):
            rows[b] = jnp.where(inside, 0.0, rows[b]) - product(rows[b], k0, pieces)
            yield
    out.append(rows[16])


def in_turn(*works):
    works = list(works)
    while works:
        for work in list(works):
            try:
                next(work)
            except StopIteration:
                works.remove(work)


def sideways(field):
    nothing = jnp.zeros((field.shape[0], 1), F32)
    left = jnp.concatenate([nothing, field[:, :-1]], axis=1)
    right = jnp.concatenate([field[:, 1:], nothing], axis=1)
    return left + right - 4.0 * field


def coupling_of(kinds, rates):
    coupling = jnp.zeros(kinds.shape, F32)
    for kind in range(4):
        coupling = jnp.where(kinds == kind, rates[kind], coupling)
    return coupling


def loop(low, high, body):
    def step(d, carry):
        body(d)
        return carry

    lax.fori_loop(low, high, step, 0)


def whole_kernel(
    x_hbm, om_hbm, psi_hbm, spec_hbm, rates, adj_hbm,
    adj_out, t_out,
    xb, psib, omb, spec, adj, yt, c_acc, k_acc, zeros,
    ar, ct, ct_pair, ct_half, ar_in, ct_in, part, z_in, done, sums, ct_part, ctz_in, edge, halo, halo_y,
    x_sem, psi_sem, small_sem,
    ar_send, ar_recv, ct_send, ct_recv, z_send, z_recv, g_send, g_recv, cz_send, cz_recv,
    h_send, h_recv, y_send, y_recv, p_send, p_recv,
):
    y, z, x, c = place()
    q = (y * XS + x) * CS + c
    me = ((y * ZS + z) * XS + x) * CS + c

    def x_copy(k):
        return pltpu.make_async_copy(
            x_hbm.at[pl.ds(k * WIDTH, WIDTH), :], xb.at[k], x_sem.at[k])

    def psi_copy(k):
        return pltpu.make_async_copy(
            psi_hbm.at[:, pl.ds(k * WIDTH, WIDTH)], psib.at[k], psi_sem.at[k])

    def fetch(k):
        x_copy(k).start()
        psi_copy(k).start()

    om_copy = pltpu.make_async_copy(om_hbm, omb, small_sem.at[0])
    spec_copy = pltpu.make_async_copy(spec_hbm, spec, small_sem.at[1])
    adj_copy = pltpu.make_async_copy(adj_hbm, adj, small_sem.at[2])
    om_copy.start()
    for i in range(AHEAD):
        fetch((i + 7) % STEPS)
    spec_copy.start()
    adj_copy.start()

    y_at = [lax.rem(y + d, YS) for d in range(YS)]
    x_at = [lax.rem(x + d, XS) for d in range(XS)]
    z_at = [lax.rem(z + d, ZS) for d in range(ZS)]
    c_at = [c, 1 - c]
    plane = [
        ((yy * XS + xx) * CS + cc, ((yy * ZS + z) * XS + xx, cc))
        for yy in y_at for xx in x_at for cc in c_at
    ][1:]
    chips = [
        (yy * XS + xx, ((yy * ZS + z) * XS + xx, c)) for yy in y_at for xx in x_at
    ][1:]
    column = [(zz, ((y * ZS + zz) * XS + x, c)) for zz in z_at[1:]]
    after, before = lax.rem(me + 1, 256), lax.rem(me + 255, 256)
    ring = [(lax.div(after, CS), lax.rem(after, CS)), (lax.div(before, CS), lax.rem(before, CS))]

    barrier = pltpu.get_barrier_semaphore()
    for to in [p[1] for p in plane + column] + ring:
        pl.semaphore_signal(barrier, inc=1, device_id=to, device_id_type=MESH)

    def remote(source, target, send, recv, to):
        return pltpu.make_async_remote_copy(
            src_ref=source, dst_ref=target, send_sem=send, recv_sem=recv,
            device_id=to, device_id_type=MESH)

    def all_of(source, target, send, recv, count):
        return remote(source.at[pl.ds(0, count)], target.at[pl.ds(0, count)], send, recv, ring[0])

    def h_copy(which):
        return remote(edge.at[which], halo.at[which], h_send.at[which], h_recv.at[which],
                      ring[which])

    def y_copy(which):
        return remote(yt.at[7 if which == 0 else 0], halo_y.at[which],
                      y_send.at[which], y_recv.at[which], ring[which])

    zeros[...] = jnp.zeros_like(zeros)
    c_acc[...] = jnp.zeros_like(c_acc)
    k_acc[...] = jnp.zeros_like(k_acc)
    om_copy.wait()

    def block(i):
        k = lax.rem(i + 7, STEPS)
        x_copy(k).wait()
        psi_copy(k).wait()
        xs = xb[k]
        ys = jnp.dot(xs, omb[...], preferred_element_type=F32)
        c_acc[...] += jnp.dot(psib[k], xs, preferred_element_type=F32)
        ys_t = ys.T
        yt[k] = ys_t
        hi = ys.astype(BF16)
        lo = (ys - hi.astype(F32)).astype(BF16)
        wide = jnp.concatenate([hi, lo], axis=1)
        k_acc[...] += jnp.dot(ys_t.astype(BF16), wide, preferred_element_type=F32)

    def pair(i):
        ks = [lax.rem(i + 7, STEPS), lax.rem(i + 8, STEPS)]
        turns = []
        for k in ks:
            x_copy(k).wait()
            psi_copy(k).wait()
        for k in ks:
            turns.append(jnp.dot(xb[k], omb[...], preferred_element_type=F32))
        both = jnp.dot(psib[ks[0]], xb[ks[0]], preferred_element_type=F32)
        grams = None
        for n, k in enumerate(ks):
            ys = turns[n]
            ys_t = ys.T
            yt[k] = ys_t
            hi = ys.astype(BF16)
            lo = (ys - hi.astype(F32)).astype(BF16)
            wide = jnp.concatenate([hi, lo], axis=1)
            here = jnp.dot(ys_t.astype(BF16), wide, preferred_element_type=F32)
            if n == 0:
                grams = here
                both = both + jnp.dot(psib[ks[1]], xb[ks[1]], preferred_element_type=F32)
            else:
                grams = grams + here
        c_acc[...] += both
        k_acc[...] += grams

    def early(i):
        fetch(lax.rem(i + 7 + AHEAD, STEPS))
        block(i)

    loop(0, 2, early)
    for i in range(2 + AHEAD, STEPS):
        fetch((i + 7) % STEPS)
    spec_copy.wait()
    adj_copy.wait()
    coupling = coupling_of(spec[...], rates)
    edge[0, 0:1] = adj[7:8, :]
    edge[0, 1:2] = adj[6:7, :]
    edge[0, 2:3] = coupling[7:8, :]
    edge[0, 3:4] = coupling[7:8, :]
    edge[1, 0:1] = adj[0:1, :]
    edge[1, 1:2] = adj[1:2, :]
    edge[1, 2:3] = coupling[0:1, :]
    edge[1, 3:4] = coupling[0:1, :]
    pl.semaphore_wait(barrier, PLANE - 1 + ZS - 1 + 2)
    for which in range(2):
        y_copy(which).start()
        h_copy(which).start()
    loop(1, STEPS // 2, lambda n: pair(2 * n))
    r = 128
    cross = k_acc[:, r:]
    gram = k_acc[:, 0:r] + (cross + cross.T)
    om_f = omb[...]
    c_all = c_acc[...]
    c_1 = c_all.astype(BF16)
    rest = c_all - c_1.astype(F32)
    c_2 = rest.astype(BF16)
    c_3 = (rest - c_2.astype(F32)).astype(BF16)
    raw = (
        jnp.dot(c_3, om_f, preferred_element_type=F32)
        + jnp.dot(c_2, om_f, preferred_element_type=F32)
        + jnp.dot(c_1, om_f, preferred_element_type=F32)
    )
    row = iota((r, r), 0)
    source = ((row >> 1) & 7) * 16 + ((row >> 4) & 3) * 4 + ((row >> 6) & 1) * 2 + (row & 1)
    perm = jnp.where(iota((r, r), 1) == source, 1.0, 0.0).astype(F32)

    def turned(at):
        piece = lax.dot_general(
            perm, c_acc[:, at * r : (at + 1) * r], (((1,), (1,)), ((), ())),
            precision=HIGH, preferred_element_type=F32)
        ct[0, 4 * at : 4 * at + 4] = piece[0:64].reshape(4, 16, 256)
        ct[1, 4 * at : 4 * at + 4] = piece[64:128].reshape(4, 16, 256)

    turned(YS - 1)
    ends = ct[1, 15, 14:16, :]
    carried = jnp.concatenate(
        [ends[i : i + 1, 64 * k : 64 * k + 64] for i in range(2) for k in range(4)], axis=0)
    mixed = jnp.concatenate([carried, gram[64:72, 64:128]], axis=1)
    for p in range(PLANE):
        ar[p, 0] = raw[8 * p : 8 * p + 4]
        ar[p, 1] = raw[8 * p + 4 : 8 * p + 8]
        ar[p, 2] = gram[4 * p : 4 * p + 4] if p not in (16, 17) else (
            mixed[0:4] if p == 16 else mixed[4:8])

    for p, to in plane:
        remote(ar.at[p], ar_in.at[q], ar_send, ar_recv, to).start()
    ar_in[q] = ar[q]
    for at in range(YS - 1):
        turned(at)
    pair_copy = remote(ct.at[1 - c], ct_pair, p_send, p_recv, (lax.axis_index("space"), 1 - c))
    pair_copy.start()
    all_of(ar, ar_in, ar_send, ar_recv, PLANE - 1).wait_recv()
    part[...] = jnp.sum(ar_in[...], axis=0)

    for zz, to in column:
        remote(part, z_in.at[z], z_send, z_recv, to).start()
    pair_copy.wait_recv()
    ct_half[...] = ct[c] + ct_pair[...]
    chip = y * XS + x
    for n, to in chips:
        remote(ct_half.at[n], ct_in.at[chip], ct_send, ct_recv, to).start()
    ct_in[chip] = ct_half[chip]
    z_in[z] = part[...]
    all_of(z_in, z_in, z_send, z_recv, ZS - 1).wait_recv()
    total = jnp.sum(z_in[...], axis=0)
    done[...] = total

    for p, to in plane:
        remote(done, sums.at[q], g_send, g_recv, to).start()
    sums[q] = total

    all_of(ct_half, ct_in, ct_send, ct_recv, YS * XS - 1).wait_recv()
    ct_sum = jnp.sum(ct_in[...], axis=0)
    for zz in range(ZS):
        ct_part[zz] = ct_sum[2 * zz : 2 * zz + 2]
    for zz, to in column:
        remote(ct_part.at[zz], ctz_in.at[z], cz_send, cz_recv, to).start()
    ctz_in[z] = ct_part[z]
    all_of(sums, sums, g_send, g_recv, PLANE - 1).wait_recv()
    all_of(ct_part, ctz_in, cz_send, cz_recv, ZS - 1).wait_recv()
    mine = jnp.sum(ctz_in[...], axis=0)

    raw = jnp.concatenate([sums[p, half] for p in range(PLANE) for half in range(2)], axis=0)
    gram_rows = [
        jnp.concatenate([sums[2 * k, 2], sums[2 * k + 1, 2]], axis=0) for k in range(16)
    ]
    mixed = gram_rows[8]
    last = jnp.concatenate([
        jnp.concatenate([mixed[4 * i + k : 4 * i + k + 1, 0:64] for k in range(4)], axis=1)
        for i in range(2)
    ], axis=0)
    mirror = jnp.concatenate(gram_rows[0:8], axis=0).T[64:72, :]
    gram_rows[8] = jnp.concatenate([mirror, mixed[:, 64:128]], axis=1)
    right = jnp.concatenate([mine, last, jnp.zeros((4, 256), F32)], axis=0)
    right = jnp.dot(right, raw, precision=HIGH)
    normal = lax.dot_general(raw, raw, (((0,), (0,)), ((), ())), precision=HIGH)
    upper, solved = [], []
    zero = zeros[...]
    in_turn(
        solve_rows([normal[8 * k : 8 * k + 8] for k in range(16)], right, zero, solved),
        upper_factor(gram_rows, zero, upper),
    )
    solved = solved[0]
    factor = jnp.concatenate(upper, axis=0)
    times = lax.dot_general(
        solved, factor, (((1,), (1,)), ((), ())), precision=HIGH
    ) * (2097152.0 ** -0.5)
    t_out[...] = times[0:2]
    columns = jnp.concatenate([solved] * 16, axis=0).T

    def state(blocks, j):
        weights = jnp.broadcast_to(columns[:, j : j + 1], (r, r))
        tiles = []
        for b in range(8):
            tiles.append(jnp.concatenate([
                jnp.sum(get(b * r) * weights, axis=0, keepdims=True) for get in blocks
            ], axis=0))
        return jnp.concatenate(tiles, axis=1)

    own = [functools.partial(lambda k, at: yt[k, :, at : at + r], k) for k in range(8)]
    y_copy(0).wait_recv()
    y_copy(1).wait_recv()
    h_copy(0).wait_recv()
    h_copy(1).wait_recv()
    outer = [functools.partial(lambda k, at: halo_y[k, :, at : at + r], k) for k in range(2)]
    first, second, edges = state(own, 3), state(own, 2), state(outer, 3)

    coupling = STEP_SIZE * coupling_of(spec[...], rates)
    field = adj[...]
    near = jnp.concatenate([halo[0, 0:1], halo[1, 0:1]], axis=0)
    far = jnp.concatenate([halo[0, 1:2], halo[1, 1:2]], axis=0)
    rate = jnp.concatenate([halo[0, 2:3], halo[1, 2:3]], axis=0) * STEP_SIZE
    inner = jnp.concatenate([field[0:1], field[7:8]], axis=0)
    side = iota((2, WIDTH), 0)
    absent = ((side == 0) & (me == 0)) | ((side == 1) & (me == 255))
    near = jnp.where(absent, 0.0, near)
    near_next = (
        near + DIFFUSION * (far + inner + sideways(near))
        + rate * (1.0 - 3.0 * edges * edges) * near
    )
    near_next = jnp.where(absent, 0.0, near_next)

    def advance(field, low, high, state):
        up = jnp.concatenate([low, field[0:7]], axis=0)
        down = jnp.concatenate([field[1:8], high], axis=0)
        return (
            field + DIFFUSION * (up + down + sideways(field))
            + coupling * (1.0 - 3.0 * state * state) * field
        )

    field = advance(field, near[0:1], near[1:2], first)
    adj_out[...] = advance(field, near_next[0:1], near_next[1:2], second)

    for which in range(2):
        h_copy(which).wait_send()
        y_copy(which).wait_send()
    all_of(ar, ar_in, ar_send, ar_recv, PLANE - 1).wait_send()
    all_of(ct_half, ct_in, ct_send, ct_recv, YS * XS - 1).wait_send()
    pair_copy.wait_send()
    all_of(sums, sums, g_send, g_recv, PLANE - 1).wait_send()
    all_of(z_in, z_in, z_send, z_recv, ZS - 1).wait_send()
    all_of(ct_part, ctz_in, cz_send, cz_recv, ZS - 1).wait_send()


def pass_kernel(adj, times, adj_out, times_out):
    adj_out[...] = adj[...]
    times_out[...] = times[...]


def shards(snapshots, range_test, test_rows, species, reaction_rates, adjoint_end):
    vmem = pl.BlockSpec(memory_space=pltpu.VMEM)
    smem = pl.BlockSpec(memory_space=pltpu.SMEM)
    hbm = pl.BlockSpec(memory_space=pl.ANY)
    dma = pltpu.SemaphoreType.DMA
    buffer = pltpu.VMEM
    adjoint, factors = pl.pallas_call(
        whole_kernel,
        in_specs=[hbm, hbm, hbm, hbm, smem, hbm],
        out_specs=[vmem] * 2,
        out_shape=[
            jax.ShapeDtypeStruct((8, WIDTH), F32),
            jax.ShapeDtypeStruct((2, 128), F32),
        ],
        scratch_shapes=[
            buffer((STEPS, WIDTH, 512), BF16),
            buffer((STEPS, 256, WIDTH), BF16),
            buffer((512, 128), BF16),
            buffer((8, WIDTH), jnp.int32),
            buffer((8, WIDTH), F32),
            buffer((STEPS, 128, WIDTH), F32),
            buffer((256, 512), F32),
            buffer((128, 256), F32),
            buffer((8, 128), F32),
            buffer((PLANE, 3, 4, 128), F32),
            buffer((2, 16, 16, 256), F32),
            buffer((16, 16, 256), F32),
            buffer((16, 16, 256), F32),
            buffer((PLANE, 3, 4, 128), F32),
            buffer((16, 16, 256), F32),
            buffer((3, 4, 128), F32),
            buffer((ZS, 3, 4, 128), F32),
            buffer((3, 4, 128), F32),
            buffer((PLANE, 3, 4, 128), F32),
            buffer((ZS, 2, 256), F32),
            buffer((ZS, 2, 256), F32),
            buffer((2, 4, WIDTH), F32),
            buffer((2, 4, WIDTH), F32),
            buffer((2, 128, WIDTH), F32),
            dma((STEPS,)), dma((STEPS,)), dma((3,)),
            *([dma] * 10),
            dma((2,)), dma((2,)), dma((2,)), dma((2,)), dma, dma,
        ],
        compiler_params=pltpu.CompilerParams(
            collective_id=0, has_side_effects=True, vmem_limit_bytes=56 << 20
        ),
        name="whole",
    )(snapshots, range_test, test_rows, species, reaction_rates, adjoint_end)
    adjoint, factors = pl.pallas_call(
        pass_kernel,
        in_specs=[vmem] * 2,
        out_specs=[vmem] * 2,
        out_shape=[
            jax.ShapeDtypeStruct((8, WIDTH), F32),
            jax.ShapeDtypeStruct((2, 128), F32),
        ],
        name="pass_on",
    )(adjoint, factors)
    return adjoint, factors.T


def solution(mesh):
    cells = ("space", "tm")
    in_specs = (P(cells, None), P(), P(None, cells), P(cells, None), P(), P(cells, None))
    out_specs = (P(cells, None), P(None, cells))
    return jax.shard_map(
        shards, mesh=mesh, in_specs=in_specs, out_specs=out_specs, check_vma=False
    )
```

```python
import functools

import jax
import jax.numpy as jnp
from jax import lax
from jax.experimental import pallas as pl
from jax.experimental.pallas import tpu as pltpu
from jax.sharding import PartitionSpec as P

DIFFUSION = 0.2
STEP_SIZE = 0.05
MESH = pl.DeviceIdType.MESH
HIGH = lax.Precision.HIGHEST
F32 = jnp.float32
BF16 = jnp.bfloat16

YS, ZS, XS, CS = 4, 8, 4, 2
PLANE = YS * XS * CS
STEPS = 8
WIDTH = 1024
AHEAD = 4


def iota(shape, dim):
    return lax.broadcasted_iota(jnp.int32, shape, dim)


def place():
    s = lax.axis_index("space")
    return (
        lax.div(s, ZS * XS), lax.rem(lax.div(s, XS), ZS), lax.rem(s, XS), lax.axis_index("tm")
    )


def lane(a, k):
    return jnp.broadcast_to(a[:, k : k + 1], (8, 128))


def sub(a, k):
    return jnp.broadcast_to(a[k : k + 1, :], (8, 128))


def product(old, k0, pieces):
    terms = [lane(old, k0 + j) * pieces[j] for j in range(8)]
    while len(terms) > 1:
        terms = [terms[i] + terms[i + 1] for i in range(0, len(terms), 2)]
    return terms[0]


def panel_steps(panel, k0, in_place, zero):
    subs, lanes = iota((8, 128), 0), iota((8, 128), 1)
    cols = [lane(panel, k0 + j) + zero for j in range(8)]
    upper = jnp.zeros((8, 128), F32)
    for i in range(8):
        here = subs == i
        pivot = sub(cols[i], i)
        inverse = 1.0 / pivot
        if in_place:
            panel = jnp.where(lanes == k0 + i, jnp.where(here, 1.0, 0.0), panel)
        else:
            upper = jnp.where(here & (lanes >= k0 + i), panel * lax.rsqrt(pivot), upper)
        row = sub(panel, i) * inverse
        panel = jnp.where(here, row, panel - cols[i] * row)
        for j in range(i + 1, 8):
            entry = sub(cols[j], i) * inverse
            cols[j] = jnp.where(here, entry, cols[j] - cols[i] * entry)
        yield
    return panel, upper


def split(value):
    one = value.astype(BF16).astype(F32)
    rest = value - one
    two = rest.astype(BF16).astype(F32)
    return one, two, rest - two


def outer(left, right):
    a, b, c = split(left)
    d, e, f = split(right)
    wide = jnp.concatenate([a, a, b, a, b, c], axis=0).astype(BF16)
    tall = jnp.concatenate([d, e, d, f, e, d], axis=0).astype(BF16)
    return lax.dot_general(
        wide, tall, (((0,), (0,)), ((), ())), preferred_element_type=F32)


def upper_factor(rows, zero, out):
    rows = list(rows)
    for k in range(16):
        k0 = 8 * k
        old = rows[k]
        panel, upper = yield from panel_steps(old, k0, False, zero)
        out.append(upper)
        if k < 15:
            pieces = [sub(panel, j) for j in range(8)]
            rows[k + 1] = rows[k + 1] - product(rows[k + 1], k0, pieces)
            yield
        if k < 14:
            update = outer(old, panel)
            for b in range(k + 2, 16):
                rows[b] = rows[b] - update[8 * b : 8 * b + 8]
            yield


def solve_rows(rows, right, zero, out):
    rows = list(rows)
    lanes = iota((8, 128), 1)
    for k in range(16):
        k0 = 8 * k
        inside = (lanes >= k0) & (lanes < k0 + 8)
        old = rows[k]
        panel, _ = yield from panel_steps(old, k0, True, zero)
        panel = jnp.where(inside, -panel, panel)
        pieces = [sub(panel, j) for j in range(8)]
        if k < 15:
            rows[k + 1] = jnp.where(inside, 0.0, rows[k + 1]) - product(rows[k + 1], k0, pieces)
            yield
        right = jnp.where(inside, 0.0, right) - product(right, k0, pieces)
        yield
        if k < 14:
            update = outer(old, panel)
            for b in range(k + 2, 16):
                rows[b] = jnp.where(inside, 0.0, rows[b]) - update[8 * b : 8 * b + 8]
            yield
    out.append(right)


def in_turn(*works):
    works = list(works)
    while works:
        for work in list(works):
            try:
                next(work)
            except StopIteration:
                works.remove(work)


def sideways(field):
    nothing = jnp.zeros((field.shape[0], 1), F32)
    left = jnp.concatenate([nothing, field[:, :-1]], axis=1)
    right = jnp.concatenate([field[:, 1:], nothing], axis=1)
    return left + right - 4.0 * field


def coupling_of(kinds, rates):
    coupling = jnp.zeros(kinds.shape, F32)
    for kind in range(4):
        coupling = jnp.where(kinds == kind, rates[kind], coupling)
    return coupling


def loop(low, high, body):
    def step(d, carry):
        body(d)
        return carry

    lax.fori_loop(low, high, step, 0)


def whole_kernel(
    x_hbm, om_hbm, psi_hbm, spec_hbm, rates, adj_hbm,
    adj_out, t_out,
    xb, psib, omb, spec, adj, yt, c_acc, k_acc, zeros,
    ar, ct, ct_pair, ct_half, ar_in, ct_in, part, z_in, done, sums, ct_part, ctz_in, edge, halo, halo_y,
    x_sem, psi_sem, small_sem,
    ar_send, ar_recv, ct_send, ct_recv, z_send, z_recv, g_send, g_recv, cz_send, cz_recv,
    h_send, h_recv, y_send, y_recv, p_send, p_recv,
):
    y, z, x, c = place()
    q = (y * XS + x) * CS + c
    me = ((y * ZS + z) * XS + x) * CS + c

    def x_copy(k):
        return pltpu.make_async_copy(
            x_hbm.at[pl.ds(k * WIDTH, WIDTH), :], xb.at[k], x_sem.at[k])

    def psi_copy(k):
        return pltpu.make_async_copy(
            psi_hbm.at[:, pl.ds(k * WIDTH, WIDTH)], psib.at[k], psi_sem.at[k])

    def fetch(k):
        x_copy(k).start()
        psi_copy(k).start()

    om_copy = pltpu.make_async_copy(om_hbm, omb, small_sem.at[0])
    spec_copy = pltpu.make_async_copy(spec_hbm, spec, small_sem.at[1])
    adj_copy = pltpu.make_async_copy(adj_hbm, adj, small_sem.at[2])
    om_copy.start()
    for i in range(AHEAD):
        fetch((i + 7) % STEPS)
    spec_copy.start()
    adj_copy.start()

    y_at = [lax.rem(y + d, YS) for d in range(YS)]
    x_at = [lax.rem(x + d, XS) for d in range(XS)]
    z_at = [lax.rem(z + d, ZS) for d in range(ZS)]
    c_at = [c, 1 - c]
    near = [(2, 2), (1, 2), (2, 1), (2, 3), (3, 2), (0, 2), (1, 1), (1, 3), (2, 0), (3, 1), (3, 3), (0, 1), (0, 3), (1, 0), (3, 0)]
    plane = [
        ((y_at[dy] * XS + x_at[dx]) * CS + cc,
         ((y_at[dy] * ZS + z) * XS + x_at[dx], cc))
        for dy, dx in near for cc in c_at
    ] + [((y * XS + x) * CS + 1 - c, (lax.axis_index("space"), 1 - c))]
    chips = [
        (y_at[dy] * XS + x_at[dx], ((y_at[dy] * ZS + z) * XS + x_at[dx], c)) for dy, dx in near
    ]
    column = [(zz, ((y * ZS + zz) * XS + x, c)) for zz in [z_at[d] for d in [4, 3, 5, 2, 6, 1, 7]]]
    after, before = lax.rem(me + 1, 256), lax.rem(me + 255, 256)
    ring = [(lax.div(after, CS), lax.rem(after, CS)), (lax.div(before, CS), lax.rem(before, CS))]

    barrier = pltpu.get_barrier_semaphore()
    for to in [p[1] for p in plane + column] + ring:
        pl.semaphore_signal(barrier, inc=1, device_id=to, device_id_type=MESH)

    def remote(source, target, send, recv, to):
        return pltpu.make_async_remote_copy(
            src_ref=source, dst_ref=target, send_sem=send, recv_sem=recv,
            device_id=to, device_id_type=MESH)

    def all_of(source, target, send, recv, count):
        return remote(source.at[pl.ds(0, count)], target.at[pl.ds(0, count)], send, recv, ring[0])

    def h_copy(which):
        return remote(edge.at[which], halo.at[which], h_send.at[which], h_recv.at[which],
                      ring[which])

    def y_copy(which):
        return remote(yt.at[7 if which == 0 else 0], halo_y.at[which],
                      y_send.at[which], y_recv.at[which], ring[which])

    zeros[...] = jnp.zeros_like(zeros)
    c_acc[...] = jnp.zeros_like(c_acc)
    k_acc[...] = jnp.zeros_like(k_acc)
    om_copy.wait()

    def block(i):
        k = lax.rem(i + 7, STEPS)
        x_copy(k).wait()
        psi_copy(k).wait()
        xs = xb[k]
        ys = jnp.dot(xs, omb[...], preferred_element_type=F32)
        c_acc[...] += jnp.dot(psib[k], xs, preferred_element_type=F32)
        ys_t = ys.T
        yt[k] = ys_t
        hi = ys.astype(BF16)
        lo = (ys - hi.astype(F32)).astype(BF16)
        wide = jnp.concatenate([hi, lo], axis=1)
        k_acc[...] += jnp.dot(ys_t.astype(BF16), wide, preferred_element_type=F32)

    def pair(i):
        ks = [lax.rem(i + 7, STEPS), lax.rem(i + 8, STEPS)]
        turns = []
        for k in ks:
            x_copy(k).wait()
            psi_copy(k).wait()
        for k in ks:
            turns.append(jnp.dot(xb[k], omb[...], preferred_element_type=F32))
        both = jnp.dot(psib[ks[0]], xb[ks[0]], preferred_element_type=F32)
        grams = None
        for n, k in enumerate(ks):
            ys = turns[n]
            ys_t = ys.T
            yt[k] = ys_t
            hi = ys.astype(BF16)
            lo = (ys - hi.astype(F32)).astype(BF16)
            wide = jnp.concatenate([hi, lo], axis=1)
            here = jnp.dot(ys_t.astype(BF16), wide, preferred_element_type=F32)
            if n == 0:
                grams = here
                both = both + jnp.dot(psib[ks[1]], xb[ks[1]], preferred_element_type=F32)
            else:
                grams = grams + here
        c_acc[...] += both
        k_acc[...] += grams

    def early(i):
        fetch(lax.rem(i + 7 + AHEAD, STEPS))
        block(i)

    loop(0, 2, early)
    for i in range(2 + AHEAD, STEPS):
        fetch((i + 7) % STEPS)
    spec_copy.wait()
    adj_copy.wait()
    coupling = coupling_of(spec[...], rates)
    edge[0, 0:1] = adj[7:8, :]
    edge[0, 1:2] = adj[6:7, :]
    edge[0, 2:3] = coupling[7:8, :]
    edge[0, 3:4] = coupling[7:8, :]
    edge[1, 0:1] = adj[0:1, :]
    edge[1, 1:2] = adj[1:2, :]
    edge[1, 2:3] = coupling[0:1, :]
    edge[1, 3:4] = coupling[0:1, :]
    pl.semaphore_wait(barrier, PLANE - 1 + ZS - 1 + 2)
    for which in range(2):
        y_copy(which).start()
        h_copy(which).start()
    loop(1, STEPS // 2, lambda n: pair(2 * n))
    r = 128
    cross = k_acc[:, r:]
    gram = k_acc[:, 0:r] + (cross + cross.T)
    om_f = omb[...]
    c_all = c_acc[...]
    c_1 = c_all.astype(BF16)
    rest = c_all - c_1.astype(F32)
    c_2 = rest.astype(BF16)
    c_3 = (rest - c_2.astype(F32)).astype(BF16)
    raw = (
        jnp.dot(c_3, om_f, preferred_element_type=F32)
        + jnp.dot(c_2, om_f, preferred_element_type=F32)
        + jnp.dot(c_1, om_f, preferred_element_type=F32)
    )
    row = iota((r, r), 0)
    source = ((row >> 1) & 7) * 16 + ((row >> 4) & 3) * 4 + ((row >> 6) & 1) * 2 + (row & 1)
    perm = jnp.where(iota((r, r), 1) == source, 1.0, 0.0).astype(F32)

    def turned(at):
        piece = lax.dot_general(
            perm, c_acc[:, at * r : (at + 1) * r], (((1,), (1,)), ((), ())),
            precision=HIGH, preferred_element_type=F32)
        ct[0, 4 * at : 4 * at + 4] = piece[0:64].reshape(4, 16, 256)
        ct[1, 4 * at : 4 * at + 4] = piece[64:128].reshape(4, 16, 256)

    turned(YS - 1)
    ends = ct[1, 15, 14:16, :]
    carried = jnp.concatenate(
        [ends[i : i + 1, 64 * k : 64 * k + 64] for i in range(2) for k in range(4)], axis=0)
    mixed = jnp.concatenate([carried, gram[64:72, 64:128]], axis=1)
    for p in range(PLANE):
        ar[p, 0] = raw[8 * p : 8 * p + 4]
        ar[p, 1] = raw[8 * p + 4 : 8 * p + 8]
        ar[p, 2] = gram[4 * p : 4 * p + 4] if p not in (16, 17) else (
            mixed[0:4] if p == 16 else mixed[4:8])

    for p, to in plane:
        remote(ar.at[p], ar_in.at[q], ar_send, ar_recv, to).start()
    ar_in[q] = ar[q]
    for at in range(YS - 1):
        turned(at)
    pair_copy = remote(ct.at[1 - c], ct_pair, p_send, p_recv, (lax.axis_index("space"), 1 - c))
    pair_copy.start()
    all_of(ar, ar_in, ar_send, ar_recv, PLANE - 1).wait_recv()
    part[...] = jnp.sum(ar_in[...], axis=0)

    for zz, to in column:
        remote(part, z_in.at[z], z_send, z_recv, to).start()
    pair_copy.wait_recv()
    ct_half[...] = ct[c] + ct_pair[...]
    chip = y * XS + x
    for n, to in chips:
        remote(ct_half.at[n], ct_in.at[chip], ct_send, ct_recv, to).start()
    ct_in[chip] = ct_half[chip]
    z_in[z] = part[...]
    all_of(z_in, z_in, z_send, z_recv, ZS - 1).wait_recv()
    total = jnp.sum(z_in[...], axis=0)
    done[...] = total

    for p, to in plane:
        remote(done, sums.at[q], g_send, g_recv, to).start()
    sums[q] = total

    all_of(ct_half, ct_in, ct_send, ct_recv, YS * XS - 1).wait_recv()
    ct_sum = jnp.sum(ct_in[...], axis=0)
    for zz in range(ZS):
        ct_part[zz] = ct_sum[2 * zz : 2 * zz + 2]
    for zz, to in column:
        remote(ct_part.at[zz], ctz_in.at[z], cz_send, cz_recv, to).start()
    ctz_in[z] = ct_part[z]
    all_of(sums, sums, g_send, g_recv, PLANE - 1).wait_recv()
    all_of(ct_part, ctz_in, cz_send, cz_recv, ZS - 1).wait_recv()
    mine = jnp.sum(ctz_in[...], axis=0)

    raw = jnp.concatenate([sums[p, half] for p in range(PLANE) for half in range(2)], axis=0)
    gram_rows = [
        jnp.concatenate([sums[2 * k, 2], sums[2 * k + 1, 2]], axis=0) for k in range(16)
    ]
    mixed = gram_rows[8]
    last = jnp.concatenate([
        jnp.concatenate([mixed[4 * i + k : 4 * i + k + 1, 0:64] for k in range(4)], axis=1)
        for i in range(2)
    ], axis=0)
    mirror = jnp.concatenate(gram_rows[0:8], axis=0).T[64:72, :]
    gram_rows[8] = jnp.concatenate([mirror, mixed[:, 64:128]], axis=1)
    right = jnp.concatenate([mine, last, jnp.zeros((4, 256), F32)], axis=0)
    right = jnp.dot(right, raw, precision=HIGH)
    normal = lax.dot_general(raw, raw, (((0,), (0,)), ((), ())), precision=HIGH)
    upper, solved = [], []
    zero = zeros[...]
    in_turn(
        solve_rows([normal[8 * k : 8 * k + 8] for k in range(16)], right, zero, solved),
        upper_factor(gram_rows, zero, upper),
    )
    solved = solved[0]
    factor = jnp.concatenate(upper, axis=0)
    times = lax.dot_general(
        solved, factor, (((1,), (1,)), ((), ())), precision=HIGH
    ) * (2097152.0 ** -0.5)
    t_out[...] = times[0:2]
    columns = jnp.concatenate([solved] * 16, axis=0).T

    def state(blocks, j):
        weights = jnp.broadcast_to(columns[:, j : j + 1], (r, r))
        tiles = []
        for b in range(8):
            tiles.append(jnp.concatenate([
                jnp.sum(get(b * r) * weights, axis=0, keepdims=True) for get in blocks
            ], axis=0))
        return jnp.concatenate(tiles, axis=1)

    own = [functools.partial(lambda k, at: yt[k, :, at : at + r], k) for k in range(8)]
    y_copy(0).wait_recv()
    y_copy(1).wait_recv()
    h_copy(0).wait_recv()
    h_copy(1).wait_recv()
    outer = [functools.partial(lambda k, at: halo_y[k, :, at : at + r], k) for k in range(2)]
    first, second, edges = state(own, 3), state(own, 2), state(outer, 3)

    coupling = STEP_SIZE * coupling_of(spec[...], rates)
    field = adj[...]
    near = jnp.concatenate([halo[0, 0:1], halo[1, 0:1]], axis=0)
    far = jnp.concatenate([halo[0, 1:2], halo[1, 1:2]], axis=0)
    rate = jnp.concatenate([halo[0, 2:3], halo[1, 2:3]], axis=0) * STEP_SIZE
    inner = jnp.concatenate([field[0:1], field[7:8]], axis=0)
    side = iota((2, WIDTH), 0)
    absent = ((side == 0) & (me == 0)) | ((side == 1) & (me == 255))
    near = jnp.where(absent, 0.0, near)
    near_next = (
        near + DIFFUSION * (far + inner + sideways(near))
        + rate * (1.0 - 3.0 * edges * edges) * near
    )
    near_next = jnp.where(absent, 0.0, near_next)

    def advance(field, low, high, state):
        up = jnp.concatenate([low, field[0:7]], axis=0)
        down = jnp.concatenate([field[1:8], high], axis=0)
        return (
            field + DIFFUSION * (up + down + sideways(field))
            + coupling * (1.0 - 3.0 * state * state) * field
        )

    field = advance(field, near[0:1], near[1:2], first)
    adj_out[...] = advance(field, near_next[0:1], near_next[1:2], second)

    for which in range(2):
        h_copy(which).wait_send()
        y_copy(which).wait_send()
    all_of(ar, ar_in, ar_send, ar_recv, PLANE - 1).wait_send()
    all_of(ct_half, ct_in, ct_send, ct_recv, YS * XS - 1).wait_send()
    pair_copy.wait_send()
    all_of(sums, sums, g_send, g_recv, PLANE - 1).wait_send()
    all_of(z_in, z_in, z_send, z_recv, ZS - 1).wait_send()
    all_of(ct_part, ctz_in, cz_send, cz_recv, ZS - 1).wait_send()


def pass_kernel(adj, times, adj_out, times_out):
    adj_out[...] = adj[...]
    times_out[...] = times[...]


def shards(snapshots, range_test, test_rows, species, reaction_rates, adjoint_end):
    vmem = pl.BlockSpec(memory_space=pltpu.VMEM)
    smem = pl.BlockSpec(memory_space=pltpu.SMEM)
    hbm = pl.BlockSpec(memory_space=pl.ANY)
    dma = pltpu.SemaphoreType.DMA
    buffer = pltpu.VMEM
    adjoint, factors = pl.pallas_call(
        whole_kernel,
        in_specs=[hbm, hbm, hbm, hbm, smem, hbm],
        out_specs=[vmem] * 2,
        out_shape=[
            jax.ShapeDtypeStruct((8, WIDTH), F32),
            jax.ShapeDtypeStruct((2, 128), F32),
        ],
        scratch_shapes=[
            buffer((STEPS, WIDTH, 512), BF16),
            buffer((STEPS, 256, WIDTH), BF16),
            buffer((512, 128), BF16),
            buffer((8, WIDTH), jnp.int32),
            buffer((8, WIDTH), F32),
            buffer((STEPS, 128, WIDTH), F32),
            buffer((256, 512), F32),
            buffer((128, 256), F32),
            buffer((8, 128), F32),
            buffer((PLANE, 3, 4, 128), F32),
            buffer((2, 16, 16, 256), F32),
            buffer((16, 16, 256), F32),
            buffer((16, 16, 256), F32),
            buffer((PLANE, 3, 4, 128), F32),
            buffer((16, 16, 256), F32),
            buffer((3, 4, 128), F32),
            buffer((ZS, 3, 4, 128), F32),
            buffer((3, 4, 128), F32),
            buffer((PLANE, 3, 4, 128), F32),
            buffer((ZS, 2, 256), F32),
            buffer((ZS, 2, 256), F32),
            buffer((2, 4, WIDTH), F32),
            buffer((2, 4, WIDTH), F32),
            buffer((2, 128, WIDTH), F32),
            dma((STEPS,)), dma((STEPS,)), dma((3,)),
            *([dma] * 10),
            dma((2,)), dma((2,)), dma((2,)), dma((2,)), dma, dma,
        ],
        compiler_params=pltpu.CompilerParams(
            collective_id=0, has_side_effects=True, vmem_limit_bytes=56 << 20
        ),
        name="whole",
    )(snapshots, range_test, test_rows, species, reaction_rates, adjoint_end)
    adjoint, factors = pl.pallas_call(
        pass_kernel,
        in_specs=[vmem] * 2,
        out_specs=[vmem] * 2,
        out_shape=[
            jax.ShapeDtypeStruct((8, WIDTH), F32),
            jax.ShapeDtypeStruct((2, 128), F32),
        ],
        name="pass_on",
    )(adjoint, factors)
    return adjoint, factors.T


def solution(mesh):
    cells = ("space", "tm")
    in_specs = (P(cells, None), P(), P(None, cells), P(cells, None), P(), P(cells, None))
    out_specs = (P(cells, None), P(None, cells))
    return jax.shard_map(
        shards, mesh=mesh, in_specs=in_specs, out_specs=out_specs, check_vma=False
    )
```

```python
import functools

import jax
import jax.numpy as jnp
from jax import lax
from jax.experimental import pallas as pl
from jax.experimental.pallas import tpu as pltpu
from jax.sharding import PartitionSpec as P

DIFFUSION = 0.2
STEP_SIZE = 0.05
MESH = pl.DeviceIdType.MESH
HIGH = lax.Precision.HIGHEST
F32 = jnp.float32
BF16 = jnp.bfloat16

YS, ZS, XS, CS = 4, 8, 4, 2
PLANE = YS * XS * CS
STEPS = 8
WIDTH = 1024
AHEAD = 4


def iota(shape, dim):
    return lax.broadcasted_iota(jnp.int32, shape, dim)


def place():
    s = lax.axis_index("space")
    return (
        lax.div(s, ZS * XS), lax.rem(lax.div(s, XS), ZS), lax.rem(s, XS), lax.axis_index("tm")
    )


def lane(a, k):
    return jnp.broadcast_to(a[:, k : k + 1], (8, 128))


def sub(a, k):
    return jnp.broadcast_to(a[k : k + 1, :], (8, 128))


def product(old, k0, pieces):
    terms = [lane(old, k0 + j) * pieces[j] for j in range(8)]
    while len(terms) > 1:
        terms = [terms[i] + terms[i + 1] for i in range(0, len(terms), 2)]
    return terms[0]


def panel_steps(panel, k0, in_place, zero):
    subs, lanes = iota((8, 128), 0), iota((8, 128), 1)
    cols = [lane(panel, k0 + j) + zero for j in range(8)]
    upper = jnp.zeros((8, 128), F32)
    for i in range(8):
        here = subs == i
        pivot = sub(cols[i], i)
        inverse = 1.0 / pivot
        if in_place:
            panel = jnp.where(lanes == k0 + i, jnp.where(here, 1.0, 0.0), panel)
        else:
            upper = jnp.where(here & (lanes >= k0 + i), panel * lax.rsqrt(pivot), upper)
        row = sub(panel, i) * inverse
        panel = jnp.where(here, row, panel - cols[i] * row)
        for j in range(i + 1, 8):
            entry = sub(cols[j], i) * inverse
            cols[j] = jnp.where(here, entry, cols[j] - cols[i] * entry)
        yield
    return panel, upper


def split(value):
    one = value.astype(BF16).astype(F32)
    rest = value - one
    two = rest.astype(BF16).astype(F32)
    return one, two, rest - two


def outer(left, right):
    a, b, c = split(left)
    d, e, f = split(right)
    wide = jnp.concatenate([a, a, b, a, b, c], axis=0).astype(BF16)
    tall = jnp.concatenate([d, e, d, f, e, d], axis=0).astype(BF16)
    return lax.dot_general(
        wide, tall, (((0,), (0,)), ((), ())), preferred_element_type=F32)


def upper_factor(rows, zero, out):
    rows = list(rows)
    for k in range(16):
        k0 = 8 * k
        old = rows[k]
        panel, upper = yield from panel_steps(old, k0, False, zero)
        out.append(upper)
        if k < 15:
            pieces = [sub(panel, j) for j in range(8)]
            rows[k + 1] = rows[k + 1] - product(rows[k + 1], k0, pieces)
            yield
        if k < 14:
            update = outer(old, panel)
            for b in range(k + 2, 16):
                rows[b] = rows[b] - update[8 * b : 8 * b + 8]
            yield


def solve_rows(rows, right, zero, out):
    rows = list(rows)
    lanes = iota((8, 128), 1)
    for k in range(16):
        k0 = 8 * k
        inside = (lanes >= k0) & (lanes < k0 + 8)
        old = rows[k]
        panel, _ = yield from panel_steps(old, k0, True, zero)
        panel = jnp.where(inside, -panel, panel)
        pieces = [sub(panel, j) for j in range(8)]
        if k < 15:
            rows[k + 1] = jnp.where(inside, 0.0, rows[k + 1]) - product(rows[k + 1], k0, pieces)
            yield
        right = jnp.where(inside, 0.0, right) - product(right, k0, pieces)
        yield
        if k < 14:
            update = outer(old, panel)
            for b in range(k + 2, 16):
                rows[b] = jnp.where(inside, 0.0, rows[b]) - update[8 * b : 8 * b + 8]
            yield
    out.append(right)


def in_turn(*works):
    works = list(works)
    while works:
        for work in list(works):
            try:
                next(work)
            except StopIteration:
                works.remove(work)


def sideways(field):
    nothing = jnp.zeros((field.shape[0], 1), F32)
    left = jnp.concatenate([nothing, field[:, :-1]], axis=1)
    right = jnp.concatenate([field[:, 1:], nothing], axis=1)
    return left + right - 4.0 * field


def coupling_of(kinds, rates):
    coupling = jnp.zeros(kinds.shape, F32)
    for kind in range(4):
        coupling = jnp.where(kinds == kind, rates[kind], coupling)
    return coupling


def loop(low, high, body):
    def step(d, carry):
        body(d)
        return carry

    lax.fori_loop(low, high, step, 0)


def whole_kernel(
    x_hbm, om_hbm, psi_hbm, spec_hbm, rates, adj_hbm,
    adj_out, t_out,
    xb, psib, omb, spec, adj, yt, c_acc, k_acc, zeros,
    ar, ct, ct_pair, ct_half, ar_in, ct_in, part, z_in, done, sums, ct_part, ctz_in, edge, halo, halo_y,
    x_sem, psi_sem, small_sem,
    ar_send, ar_recv, ct_send, ct_recv, z_send, z_recv, g_send, g_recv, cz_send, cz_recv,
    h_send, h_recv, y_send, y_recv, p_send, p_recv,
):
    y, z, x, c = place()
    q = (y * XS + x) * CS + c
    me = ((y * ZS + z) * XS + x) * CS + c

    def x_copy(k):
        return pltpu.make_async_copy(
            x_hbm.at[pl.ds(k * WIDTH, WIDTH), :], xb.at[k], x_sem.at[k])

    def psi_copy(k):
        return pltpu.make_async_copy(
            psi_hbm.at[:, pl.ds(k * WIDTH, WIDTH)], psib.at[k], psi_sem.at[k])

    def fetch(k):
        x_copy(k).start()
        psi_copy(k).start()

    om_copy = pltpu.make_async_copy(om_hbm, omb, small_sem.at[0])
    spec_copy = pltpu.make_async_copy(spec_hbm, spec, small_sem.at[1])
    adj_copy = pltpu.make_async_copy(adj_hbm, adj, small_sem.at[2])
    om_copy.start()
    for i in range(AHEAD):
        fetch((i + 7) % STEPS)
    spec_copy.start()
    adj_copy.start()

    y_at = [lax.rem(y + d, YS) for d in range(YS)]
    x_at = [lax.rem(x + d, XS) for d in range(XS)]
    z_at = [lax.rem(z + d, ZS) for d in range(ZS)]
    c_at = [c, 1 - c]
    near = [(2, 2), (1, 2), (2, 1), (2, 3), (3, 2), (0, 2), (1, 1), (1, 3), (2, 0), (3, 1), (3, 3), (0, 1), (0, 3), (1, 0), (3, 0)]
    plane = [
        ((y_at[dy] * XS + x_at[dx]) * CS + cc,
         ((y_at[dy] * ZS + z) * XS + x_at[dx], cc))
        for dy, dx in near for cc in c_at
    ] + [((y * XS + x) * CS + 1 - c, (lax.axis_index("space"), 1 - c))]
    chips = [
        (y_at[dy] * XS + x_at[dx], ((y_at[dy] * ZS + z) * XS + x_at[dx], c)) for dy, dx in near
    ]
    column = [(zz, ((y * ZS + zz) * XS + x, c)) for zz in [z_at[d] for d in [4, 3, 5, 2, 6, 1, 7]]]
    after, before = lax.rem(me + 1, 256), lax.rem(me + 255, 256)
    ring = [(lax.div(after, CS), lax.rem(after, CS)), (lax.div(before, CS), lax.rem(before, CS))]

    barrier = pltpu.get_barrier_semaphore()
    for to in [p[1] for p in plane + column] + ring:
        pl.semaphore_signal(barrier, inc=1, device_id=to, device_id_type=MESH)

    def remote(source, target, send, recv, to):
        return pltpu.make_async_remote_copy(
            src_ref=source, dst_ref=target, send_sem=send, recv_sem=recv,
            device_id=to, device_id_type=MESH)

    def all_of(source, target, send, recv, count):
        return remote(source.at[pl.ds(0, count)], target.at[pl.ds(0, count)], send, recv, ring[0])

    def h_copy(which):
        return remote(edge.at[which], halo.at[which], h_send.at[which], h_recv.at[which],
                      ring[which])

    def y_copy(which):
        return remote(yt.at[7 if which == 0 else 0], halo_y.at[which],
                      y_send.at[which], y_recv.at[which], ring[which])

    zeros[...] = jnp.zeros_like(zeros)
    c_acc[...] = jnp.zeros_like(c_acc)
    k_acc[...] = jnp.zeros_like(k_acc)
    om_copy.wait()

    def block(i):
        k = lax.rem(i + 7, STEPS)
        x_copy(k).wait()
        psi_copy(k).wait()
        xs = xb[k]
        ys = jnp.dot(xs, omb[...], preferred_element_type=F32)
        c_acc[...] += jnp.dot(psib[k], xs, preferred_element_type=F32)
        ys_t = ys.T
        yt[k] = ys_t
        hi = ys.astype(BF16)
        lo = (ys - hi.astype(F32)).astype(BF16)
        wide = jnp.concatenate([hi, lo], axis=1)
        k_acc[...] += jnp.dot(ys_t.astype(BF16), wide, preferred_element_type=F32)

    def pair(i):
        ks = [lax.rem(i + 7, STEPS), lax.rem(i + 8, STEPS)]
        turns = []
        for k in ks:
            x_copy(k).wait()
            psi_copy(k).wait()
        for k in ks:
            turns.append(jnp.dot(xb[k], omb[...], preferred_element_type=F32))
        both = jnp.dot(psib[ks[0]], xb[ks[0]], preferred_element_type=F32)
        grams = None
        for n, k in enumerate(ks):
            ys = turns[n]
            ys_t = ys.T
            yt[k] = ys_t
            hi = ys.astype(BF16)
            lo = (ys - hi.astype(F32)).astype(BF16)
            wide = jnp.concatenate([hi, lo], axis=1)
            here = jnp.dot(ys_t.astype(BF16), wide, preferred_element_type=F32)
            if n == 0:
                grams = here
                both = both + jnp.dot(psib[ks[1]], xb[ks[1]], preferred_element_type=F32)
            else:
                grams = grams + here
        c_acc[...] += both
        k_acc[...] += grams

    def early(i):
        fetch(lax.rem(i + 7 + AHEAD, STEPS))
        block(i)

    loop(0, 2, early)
    for i in range(2 + AHEAD, STEPS):
        fetch((i + 7) % STEPS)
    spec_copy.wait()
    adj_copy.wait()
    coupling = coupling_of(spec[...], rates)
    edge[0, 0:1] = adj[7:8, :]
    edge[0, 1:2] = adj[6:7, :]
    edge[0, 2:3] = coupling[7:8, :]
    edge[0, 3:4] = coupling[7:8, :]
    edge[1, 0:1] = adj[0:1, :]
    edge[1, 1:2] = adj[1:2, :]
    edge[1, 2:3] = coupling[0:1, :]
    edge[1, 3:4] = coupling[0:1, :]
    pl.semaphore_wait(barrier, PLANE - 1 + ZS - 1 + 2)
    for which in range(2):
        y_copy(which).start()
        h_copy(which).start()
    loop(1, STEPS // 2, lambda n: pair(2 * n))
    r = 128
    cross = k_acc[:, r:]
    gram = k_acc[:, 0:r] + (cross + cross.T)
    om_f = omb[...]
    c_all = c_acc[...]
    c_1 = c_all.astype(BF16)
    rest = c_all - c_1.astype(F32)
    c_2 = rest.astype(BF16)
    c_3 = (rest - c_2.astype(F32)).astype(BF16)
    raw = (
        jnp.dot(c_3, om_f, preferred_element_type=F32)
        + jnp.dot(c_2, om_f, preferred_element_type=F32)
        + jnp.dot(c_1, om_f, preferred_element_type=F32)
    )
    row = iota((r, r), 0)
    source = ((row >> 1) & 7) * 16 + ((row >> 4) & 3) * 4 + ((row >> 6) & 1) * 2 + (row & 1)
    perm = jnp.where(iota((r, r), 1) == source, 1.0, 0.0).astype(F32)

    def turned(at):
        piece = lax.dot_general(
            perm, c_acc[:, at * r : (at + 1) * r], (((1,), (1,)), ((), ())),
            precision=HIGH, preferred_element_type=F32)
        ct[0, 4 * at : 4 * at + 4] = piece[0:64].reshape(4, 16, 256)
        ct[1, 4 * at : 4 * at + 4] = piece[64:128].reshape(4, 16, 256)

    turned(YS - 1)
    ends = ct[1, 15, 14:16, :]
    carried = jnp.concatenate(
        [ends[i : i + 1, 64 * k : 64 * k + 64] for i in range(2) for k in range(4)], axis=0)
    mixed = jnp.concatenate([carried, gram[64:72, 64:128]], axis=1)
    for p in range(PLANE):
        ar[p, 0] = raw[8 * p : 8 * p + 4]
        ar[p, 1] = raw[8 * p + 4 : 8 * p + 8]
        ar[p, 2] = gram[4 * p : 4 * p + 4] if p not in (16, 17) else (
            mixed[0:4] if p == 16 else mixed[4:8])

    for p, to in plane:
        remote(ar.at[p], ar_in.at[q], ar_send, ar_recv, to).start()
    ar_in[q] = ar[q]
    for at in range(YS - 1):
        turned(at)
    pair_copy = remote(ct.at[1 - c], ct_pair, p_send, p_recv, (lax.axis_index("space"), 1 - c))
    pair_copy.start()
    all_of(ar, ar_in, ar_send, ar_recv, PLANE - 1).wait_recv()
    part[...] = jnp.sum(ar_in[...], axis=0)

    for zz, to in column:
        remote(part, z_in.at[z], z_send, z_recv, to).start()
    pair_copy.wait_recv()
    ct_half[...] = ct[c] + ct_pair[...]
    chip = y * XS + x
    for n, to in chips:
        remote(ct_half.at[n], ct_in.at[chip], ct_send, ct_recv, to).start()
    ct_in[chip] = ct_half[chip]
    z_in[z] = part[...]
    all_of(z_in, z_in, z_send, z_recv, ZS - 1).wait_recv()
    total = jnp.sum(z_in[...], axis=0)
    done[...] = total

    for p, to in plane:
        remote(done, sums.at[q], g_send, g_recv, to).start()
    sums[q] = total

    all_of(ct_half, ct_in, ct_send, ct_recv, YS * XS - 1).wait_recv()
    ct_sum = jnp.sum(ct_in[...], axis=0)
    for zz in range(ZS):
        ct_part[zz] = ct_sum[2 * zz : 2 * zz + 2]
    for zz, to in column:
        remote(ct_part.at[zz], ctz_in.at[z], cz_send, cz_recv, to).start()
    ctz_in[z] = ct_part[z]
    all_of(sums, sums, g_send, g_recv, PLANE - 1).wait_recv()
    all_of(ct_part, ctz_in, cz_send, cz_recv, ZS - 1).wait_recv()
    mine = jnp.sum(ctz_in[...], axis=0)

    raw = jnp.concatenate([sums[p, half] for p in range(PLANE) for half in range(2)], axis=0)
    gram_rows = [
        jnp.concatenate([sums[2 * k, 2], sums[2 * k + 1, 2]], axis=0) for k in range(16)
    ]
    mixed = gram_rows[8]
    last = jnp.concatenate([
        jnp.concatenate([mixed[4 * i + k : 4 * i + k + 1, 0:64] for k in range(4)], axis=1)
        for i in range(2)
    ], axis=0)
    mirror = jnp.concatenate(gram_rows[0:8], axis=0).T[64:72, :]
    gram_rows[8] = jnp.concatenate([mirror, mixed[:, 64:128]], axis=1)
    right = jnp.concatenate([mine, last, jnp.zeros((4, 256), F32)], axis=0)
    right = jnp.dot(right, raw, precision=HIGH)
    normal = lax.dot_general(raw, raw, (((0,), (0,)), ((), ())), precision=HIGH)
    upper, solved = [], []
    zero = zeros[...]
    in_turn(
        solve_rows([normal[8 * k : 8 * k + 8] for k in range(16)], right, zero, solved),
        upper_factor(gram_rows, zero, upper),
    )
    solved = solved[0]
    factor = jnp.concatenate(upper, axis=0)
    times = lax.dot_general(
        solved, factor, (((1,), (1,)), ((), ())), precision=HIGH
    ) * (2097152.0 ** -0.5)
    t_out[...] = times[0:2]
    columns = jnp.concatenate([solved] * 16, axis=0).T

    def state(blocks, j):
        weights = jnp.broadcast_to(columns[:, j : j + 1], (r, r))
        tiles = []
        for b in range(8):
            tiles.append(jnp.concatenate([
                jnp.sum(get(b * r) * weights, axis=0, keepdims=True) for get in blocks
            ], axis=0))
        return jnp.concatenate(tiles, axis=1)

    own = [functools.partial(lambda k, at: yt[k, :, at : at + r], k) for k in range(8)]
    y_copy(0).wait_recv()
    y_copy(1).wait_recv()
    h_copy(0).wait_recv()
    h_copy(1).wait_recv()
    outer = [functools.partial(lambda k, at: halo_y[k, :, at : at + r], k) for k in range(2)]
    first, second, edges = state(own, 3), state(own, 2), state(outer, 3)

    coupling = STEP_SIZE * coupling_of(spec[...], rates)
    field = adj[...]
    near = jnp.concatenate([halo[0, 0:1], halo[1, 0:1]], axis=0)
    far = jnp.concatenate([halo[0, 1:2], halo[1, 1:2]], axis=0)
    rate = jnp.concatenate([halo[0, 2:3], halo[1, 2:3]], axis=0) * STEP_SIZE
    inner = jnp.concatenate([field[0:1], field[7:8]], axis=0)
    side = iota((2, WIDTH), 0)
    absent = ((side == 0) & (me == 0)) | ((side == 1) & (me == 255))
    near = jnp.where(absent, 0.0, near)
    near_next = (
        near + DIFFUSION * (far + inner + sideways(near))
        + rate * (1.0 - 3.0 * edges * edges) * near
    )
    near_next = jnp.where(absent, 0.0, near_next)

    def advance(field, low, high, state):
        up = jnp.concatenate([low, field[0:7]], axis=0)
        down = jnp.concatenate([field[1:8], high], axis=0)
        return (
            field + DIFFUSION * (up + down + sideways(field))
            + coupling * (1.0 - 3.0 * state * state) * field
        )

    field = advance(field, near[0:1], near[1:2], first)
    adj_out[...] = advance(field, near_next[0:1], near_next[1:2], second)

    for which in range(2):
        h_copy(which).wait_send()
        y_copy(which).wait_send()
    all_of(ar, ar_in, ar_send, ar_recv, PLANE - 1).wait_send()
    all_of(ct_half, ct_in, ct_send, ct_recv, YS * XS - 1).wait_send()
    pair_copy.wait_send()
    all_of(sums, sums, g_send, g_recv, PLANE - 1).wait_send()
    all_of(z_in, z_in, z_send, z_recv, ZS - 1).wait_send()
    all_of(ct_part, ctz_in, cz_send, cz_recv, ZS - 1).wait_send()


def pass_kernel(adj, times, adj_out, times_out):
    adj_out[...] = adj[...]
    times_out[...] = times[...]


def shards(snapshots, range_test, test_rows, species, reaction_rates, adjoint_end):
    vmem = pl.BlockSpec(memory_space=pltpu.VMEM)
    smem = pl.BlockSpec(memory_space=pltpu.SMEM)
    hbm = pl.BlockSpec(memory_space=pl.ANY)
    dma = pltpu.SemaphoreType.DMA
    buffer = pltpu.VMEM
    adjoint, factors = pl.pallas_call(
        whole_kernel,
        in_specs=[hbm, hbm, hbm, hbm, smem, hbm],
        out_specs=[vmem] * 2,
        out_shape=[
            pltpu.VMEM((8, WIDTH), F32),
            pltpu.VMEM((2, 128), F32),
        ],
        scratch_shapes=[
            buffer((STEPS, WIDTH, 512), BF16),
            buffer((STEPS, 256, WIDTH), BF16),
            buffer((512, 128), BF16),
            buffer((8, WIDTH), jnp.int32),
            buffer((8, WIDTH), F32),
            buffer((STEPS, 128, WIDTH), F32),
            buffer((256, 512), F32),
            buffer((128, 256), F32),
            buffer((8, 128), F32),
            buffer((PLANE, 3, 4, 128), F32),
            buffer((2, 16, 16, 256), F32),
            buffer((16, 16, 256), F32),
            buffer((16, 16, 256), F32),
            buffer((PLANE, 3, 4, 128), F32),
            buffer((16, 16, 256), F32),
            buffer((3, 4, 128), F32),
            buffer((ZS, 3, 4, 128), F32),
            buffer((3, 4, 128), F32),
            buffer((PLANE, 3, 4, 128), F32),
            buffer((ZS, 2, 256), F32),
            buffer((ZS, 2, 256), F32),
            buffer((2, 4, WIDTH), F32),
            buffer((2, 4, WIDTH), F32),
            buffer((2, 128, WIDTH), F32),
            dma((STEPS,)), dma((STEPS,)), dma((3,)),
            *([dma] * 10),
            dma((2,)), dma((2,)), dma((2,)), dma((2,)), dma, dma,
        ],
        compiler_params=pltpu.CompilerParams(
            collective_id=0, has_side_effects=True, vmem_limit_bytes=56 << 20
        ),
        name="whole",
    )(snapshots, range_test, test_rows, species, reaction_rates, adjoint_end)
    adjoint, factors = pl.pallas_call(
        pass_kernel,
        in_specs=[vmem] * 2,
        out_specs=[vmem] * 2,
        out_shape=[
            jax.ShapeDtypeStruct((8, WIDTH), F32),
            jax.ShapeDtypeStruct((2, 128), F32),
        ],
        name="pass_on",
    )(
        pltpu.with_memory_space_constraint(adjoint, pltpu.VMEM),
        pltpu.with_memory_space_constraint(factors, pltpu.VMEM),
    )
    return adjoint, factors.T


def solution(mesh):
    cells = ("space", "tm")
    in_specs = (P(cells, None), P(), P(None, cells), P(cells, None), P(), P(cells, None))
    out_specs = (P(cells, None), P(None, cells))
    return jax.shard_map(
        shards, mesh=mesh, in_specs=in_specs, out_specs=out_specs, check_vma=False
    )
```

```python
import functools

import jax
import jax.numpy as jnp
from jax import lax
from jax.experimental import pallas as pl
from jax.experimental.pallas import tpu as pltpu
from jax.sharding import PartitionSpec as P

DIFFUSION = 0.2
STEP_SIZE = 0.05
MESH = pl.DeviceIdType.MESH
HIGH = lax.Precision.HIGHEST
F32 = jnp.float32
BF16 = jnp.bfloat16

YS, ZS, XS, CS = 4, 8, 4, 2
PLANE = YS * XS * CS
STEPS = 8
WIDTH = 1024
AHEAD = 4


def iota(shape, dim):
    return lax.broadcasted_iota(jnp.int32, shape, dim)


def place():
    s = lax.axis_index("space")
    return (
        lax.div(s, ZS * XS), lax.rem(lax.div(s, XS), ZS), lax.rem(s, XS), lax.axis_index("tm")
    )


def lane(a, k):
    return jnp.broadcast_to(a[:, k : k + 1], (8, 128))


def sub(a, k):
    return jnp.broadcast_to(a[k : k + 1, :], (8, 128))


def product(old, k0, pieces):
    terms = [lane(old, k0 + j) * pieces[j] for j in range(8)]
    while len(terms) > 1:
        terms = [terms[i] + terms[i + 1] for i in range(0, len(terms), 2)]
    return terms[0]


def panel_steps(panel, k0, in_place, zero):
    subs, lanes = iota((8, 128), 0), iota((8, 128), 1)
    cols = [lane(panel, k0 + j) + zero for j in range(8)]
    upper = jnp.zeros((8, 128), F32)
    for i in range(8):
        here = subs == i
        pivot = sub(cols[i], i)
        inverse = 1.0 / pivot
        if in_place:
            panel = jnp.where(lanes == k0 + i, jnp.where(here, 1.0, 0.0), panel)
        else:
            upper = jnp.where(here & (lanes >= k0 + i), panel * lax.rsqrt(pivot), upper)
        row = sub(panel, i) * inverse
        panel = jnp.where(here, row, panel - cols[i] * row)
        for j in range(i + 1, 8):
            entry = sub(cols[j], i) * inverse
            cols[j] = jnp.where(here, entry, cols[j] - cols[i] * entry)
        yield
    return panel, upper


def split(value):
    one = value.astype(BF16).astype(F32)
    rest = value - one
    two = rest.astype(BF16).astype(F32)
    return one, two, rest - two


def outer(left, right):
    a, b, c = split(left)
    d, e, f = split(right)
    wide = jnp.concatenate([a, a, b, a, b, c], axis=0).astype(BF16)
    tall = jnp.concatenate([d, e, d, f, e, d], axis=0).astype(BF16)
    return lax.dot_general(
        wide, tall, (((0,), (0,)), ((), ())), preferred_element_type=F32)


def upper_factor(rows, zero, out):
    rows = list(rows)
    for k in range(16):
        k0 = 8 * k
        old = rows[k]
        panel, upper = yield from panel_steps(old, k0, False, zero)
        out.append(upper)
        if k < 15:
            pieces = [sub(panel, j) for j in range(8)]
            rows[k + 1] = rows[k + 1] - product(rows[k + 1], k0, pieces)
            yield
        if k < 14:
            update = outer(old, panel)
            for b in range(k + 2, 16):
                rows[b] = rows[b] - update[8 * b : 8 * b + 8]
            yield


def solve_rows(rows, right, zero, out):
    rows = list(rows)
    lanes = iota((8, 128), 1)
    for k in range(16):
        k0 = 8 * k
        inside = (lanes >= k0) & (lanes < k0 + 8)
        old = rows[k]
        panel, _ = yield from panel_steps(old, k0, True, zero)
        panel = jnp.where(inside, -panel, panel)
        pieces = [sub(panel, j) for j in range(8)]
        if k < 15:
            rows[k + 1] = jnp.where(inside, 0.0, rows[k + 1]) - product(rows[k + 1], k0, pieces)
            yield
        right = jnp.where(inside, 0.0, right) - product(right, k0, pieces)
        yield
        if k < 14:
            update = outer(old, panel)
            for b in range(k + 2, 16):
                rows[b] = jnp.where(inside, 0.0, rows[b]) - update[8 * b : 8 * b + 8]
            yield
    out.append(right)


def in_turn(*works):
    works = list(works)
    while works:
        for work in list(works):
            try:
                next(work)
            except StopIteration:
                works.remove(work)


def sideways(field):
    nothing = jnp.zeros((field.shape[0], 1), F32)
    left = jnp.concatenate([nothing, field[:, :-1]], axis=1)
    right = jnp.concatenate([field[:, 1:], nothing], axis=1)
    return left + right - 4.0 * field


def coupling_of(kinds, rates):
    coupling = jnp.zeros(kinds.shape, F32)
    for kind in range(4):
        coupling = jnp.where(kinds == kind, rates[kind], coupling)
    return coupling


def loop(low, high, body):
    def step(d, carry):
        body(d)
        return carry

    lax.fori_loop(low, high, step, 0)


def whole_kernel(
    x_hbm, om_hbm, psi_hbm, spec_hbm, rates, adj_hbm,
    adj_out, t_out,
    xb, psib, omb, spec, adj, yt, c_acc, k_acc, zeros,
    ar, ct, ct_pair, ct_half, ar_in, ct_in, part, z_in, done, sums, ct_part, ctz_in, edge, halo, halo_y,
    x_sem, psi_sem, small_sem,
    ar_send, ar_recv, ct_send, ct_recv, z_send, z_recv, g_send, g_recv, cz_send, cz_recv,
    h_send, h_recv, y_send, y_recv, p_send, p_recv,
):
    y, z, x, c = place()
    q = (y * XS + x) * CS + c
    me = ((y * ZS + z) * XS + x) * CS + c

    def x_copy(k):
        return pltpu.make_async_copy(
            x_hbm.at[pl.ds(k * WIDTH, WIDTH), :], xb.at[k], x_sem.at[k])

    def psi_copy(k):
        return pltpu.make_async_copy(
            psi_hbm.at[:, pl.ds(k * WIDTH, WIDTH)], psib.at[k], psi_sem.at[k])

    def fetch(k):
        x_copy(k).start()
        psi_copy(k).start()

    om_copy = pltpu.make_async_copy(om_hbm, omb, small_sem.at[0])
    spec_copy = pltpu.make_async_copy(spec_hbm, spec, small_sem.at[1])
    adj_copy = pltpu.make_async_copy(adj_hbm, adj, small_sem.at[2])
    om_copy.start()
    for i in range(AHEAD):
        fetch((i + 7) % STEPS)
    spec_copy.start()
    adj_copy.start()

    y_at = [lax.rem(y + d, YS) for d in range(YS)]
    x_at = [lax.rem(x + d, XS) for d in range(XS)]
    z_at = [lax.rem(z + d, ZS) for d in range(ZS)]
    c_at = [c, 1 - c]
    near = [(2, 2), (1, 2), (2, 1), (2, 3), (3, 2), (0, 2), (1, 1), (1, 3), (2, 0), (3, 1), (3, 3), (0, 1), (0, 3), (1, 0), (3, 0)]
    plane = [
        ((y_at[dy] * XS + x_at[dx]) * CS + cc,
         ((y_at[dy] * ZS + z) * XS + x_at[dx], cc))
        for dy, dx in near for cc in c_at
    ] + [((y * XS + x) * CS + 1 - c, (lax.axis_index("space"), 1 - c))]
    chips = [
        (y_at[dy] * XS + x_at[dx], ((y_at[dy] * ZS + z) * XS + x_at[dx], c)) for dy, dx in near
    ]
    column = [(zz, ((y * ZS + zz) * XS + x, c)) for zz in [z_at[d] for d in [4, 3, 5, 2, 6, 1, 7]]]
    after, before = lax.rem(me + 1, 256), lax.rem(me + 255, 256)
    ring = [(lax.div(after, CS), lax.rem(after, CS)), (lax.div(before, CS), lax.rem(before, CS))]

    barrier = pltpu.get_barrier_semaphore()
    for to in [p[1] for p in plane + column] + ring:
        pl.semaphore_signal(barrier, inc=1, device_id=to, device_id_type=MESH)

    def remote(source, target, send, recv, to):
        return pltpu.make_async_remote_copy(
            src_ref=source, dst_ref=target, send_sem=send, recv_sem=recv,
            device_id=to, device_id_type=MESH)

    def all_of(source, target, send, recv, count):
        return remote(source.at[pl.ds(0, count)], target.at[pl.ds(0, count)], send, recv, ring[0])

    def h_copy(which):
        return remote(edge.at[which], halo.at[which], h_send.at[which], h_recv.at[which],
                      ring[which])

    def y_copy(which, half):
        rows = pl.ds(64 * half, 64)
        return remote(yt.at[7 if which == 0 else 0, rows], halo_y.at[which, rows],
                      y_send.at[2 * half + which], y_recv.at[2 * half + which], ring[which])

    zeros[...] = jnp.zeros_like(zeros)
    c_acc[...] = jnp.zeros_like(c_acc)
    k_acc[...] = jnp.zeros_like(k_acc)
    om_copy.wait()

    def block(i):
        k = lax.rem(i + 7, STEPS)
        x_copy(k).wait()
        psi_copy(k).wait()
        xs = xb[k]
        ys = jnp.dot(xs, omb[...], preferred_element_type=F32)
        c_acc[...] += jnp.dot(psib[k], xs, preferred_element_type=F32)
        ys_t = ys.T
        yt[k] = ys_t
        hi = ys.astype(BF16)
        lo = (ys - hi.astype(F32)).astype(BF16)
        wide = jnp.concatenate([hi, lo], axis=1)
        k_acc[...] += jnp.dot(ys_t.astype(BF16), wide, preferred_element_type=F32)

    def pair(i):
        ks = [lax.rem(i + 7, STEPS), lax.rem(i + 8, STEPS)]
        turns = []
        for k in ks:
            x_copy(k).wait()
            psi_copy(k).wait()
        for k in ks:
            turns.append(jnp.dot(xb[k], omb[...], preferred_element_type=F32))
        both = jnp.dot(psib[ks[0]], xb[ks[0]], preferred_element_type=F32)
        grams = None
        for n, k in enumerate(ks):
            ys = turns[n]
            ys_t = ys.T
            yt[k] = ys_t
            hi = ys.astype(BF16)
            lo = (ys - hi.astype(F32)).astype(BF16)
            wide = jnp.concatenate([hi, lo], axis=1)
            here = jnp.dot(ys_t.astype(BF16), wide, preferred_element_type=F32)
            if n == 0:
                grams = here
                both = both + jnp.dot(psib[ks[1]], xb[ks[1]], preferred_element_type=F32)
            else:
                grams = grams + here
        c_acc[...] += both
        k_acc[...] += grams

    def early(i):
        fetch(lax.rem(i + 7 + AHEAD, STEPS))
        block(i)

    loop(0, 2, early)
    for i in range(2 + AHEAD, STEPS):
        fetch((i + 7) % STEPS)
    spec_copy.wait()
    adj_copy.wait()
    coupling = coupling_of(spec[...], rates)
    edge[0, 0:1] = adj[7:8, :]
    edge[0, 1:2] = adj[6:7, :]
    edge[0, 2:3] = coupling[7:8, :]
    edge[0, 3:4] = coupling[7:8, :]
    edge[1, 0:1] = adj[0:1, :]
    edge[1, 1:2] = adj[1:2, :]
    edge[1, 2:3] = coupling[0:1, :]
    edge[1, 3:4] = coupling[0:1, :]
    pl.semaphore_wait(barrier, PLANE - 1 + ZS - 1 + 2)
    for which in range(2):
        y_copy(which, 0).start()
        h_copy(which).start()
    loop(1, STEPS // 2, lambda n: pair(2 * n))
    r = 128
    cross = k_acc[:, r:]
    gram = k_acc[:, 0:r] + (cross + cross.T)
    om_f = omb[...]
    c_all = c_acc[...]
    c_1 = c_all.astype(BF16)
    rest = c_all - c_1.astype(F32)
    c_2 = rest.astype(BF16)
    c_3 = (rest - c_2.astype(F32)).astype(BF16)
    raw = (
        jnp.dot(c_3, om_f, preferred_element_type=F32)
        + jnp.dot(c_2, om_f, preferred_element_type=F32)
        + jnp.dot(c_1, om_f, preferred_element_type=F32)
    )
    row = iota((r, r), 0)
    source = ((row >> 1) & 7) * 16 + ((row >> 4) & 3) * 4 + ((row >> 6) & 1) * 2 + (row & 1)
    perm = jnp.where(iota((r, r), 1) == source, 1.0, 0.0).astype(F32)

    def turned(at):
        piece = lax.dot_general(
            perm, c_acc[:, at * r : (at + 1) * r], (((1,), (1,)), ((), ())),
            precision=HIGH, preferred_element_type=F32)
        ct[0, 4 * at : 4 * at + 4] = piece[0:64].reshape(4, 16, 256)
        ct[1, 4 * at : 4 * at + 4] = piece[64:128].reshape(4, 16, 256)

    ends = c_acc[:, 3 * r : 4 * r].T[r - 2 : r, :]
    carried = jnp.concatenate(
        [ends[i : i + 1, 64 * k : 64 * k + 64] for i in range(2) for k in range(4)], axis=0)
    mixed = jnp.concatenate([carried, gram[64:72, 64:128]], axis=1)
    for p in range(PLANE):
        ar[p, 0] = raw[8 * p : 8 * p + 4]
        ar[p, 1] = raw[8 * p + 4 : 8 * p + 8]
        ar[p, 2] = gram[4 * p : 4 * p + 4] if p not in (16, 17) else (
            mixed[0:4] if p == 16 else mixed[4:8])

    for p, to in plane:
        remote(ar.at[p], ar_in.at[q], ar_send, ar_recv, to).start()
    ar_in[q] = ar[q]
    for at in range(YS):
        turned(at)
    pair_copy = remote(ct.at[1 - c], ct_pair, p_send, p_recv, (lax.axis_index("space"), 1 - c))
    pair_copy.start()
    all_of(ar, ar_in, ar_send, ar_recv, PLANE - 1).wait_recv()
    part[...] = jnp.sum(ar_in[...], axis=0)

    for zz, to in column:
        remote(part, z_in.at[z], z_send, z_recv, to).start()
    pair_copy.wait_recv()
    ct_half[...] = ct[c] + ct_pair[...]
    chip = y * XS + x
    for n, to in chips:
        remote(ct_half.at[n], ct_in.at[chip], ct_send, ct_recv, to).start()
    ct_in[chip] = ct_half[chip]
    z_in[z] = part[...]
    all_of(z_in, z_in, z_send, z_recv, ZS - 1).wait_recv()
    total = jnp.sum(z_in[...], axis=0)
    done[...] = total

    for p, to in plane:
        remote(done, sums.at[q], g_send, g_recv, to).start()
    sums[q] = total

    all_of(ct_half, ct_in, ct_send, ct_recv, YS * XS - 1).wait_recv()
    ct_sum = jnp.sum(ct_in[...], axis=0)
    for zz in range(ZS):
        ct_part[zz] = ct_sum[2 * zz : 2 * zz + 2]
    for zz, to in column:
        remote(ct_part.at[zz], ctz_in.at[z], cz_send, cz_recv, to).start()
    ctz_in[z] = ct_part[z]
    for which in range(2):
        y_copy(which, 1).start()
    all_of(sums, sums, g_send, g_recv, PLANE - 1).wait_recv()
    all_of(ct_part, ctz_in, cz_send, cz_recv, ZS - 1).wait_recv()
    mine = jnp.sum(ctz_in[...], axis=0)

    raw = jnp.concatenate([sums[p, half] for p in range(PLANE) for half in range(2)], axis=0)
    gram_rows = [
        jnp.concatenate([sums[2 * k, 2], sums[2 * k + 1, 2]], axis=0) for k in range(16)
    ]
    mixed = gram_rows[8]
    last = jnp.concatenate([
        jnp.concatenate([mixed[4 * i + k : 4 * i + k + 1, 0:64] for k in range(4)], axis=1)
        for i in range(2)
    ], axis=0)
    mirror = jnp.concatenate(gram_rows[0:8], axis=0).T[64:72, :]
    gram_rows[8] = jnp.concatenate([mirror, mixed[:, 64:128]], axis=1)
    right = jnp.concatenate([mine, last, jnp.zeros((4, 256), F32)], axis=0)
    right = jnp.dot(right, raw, precision=HIGH)
    normal = lax.dot_general(raw, raw, (((0,), (0,)), ((), ())), precision=HIGH)
    upper, solved = [], []
    zero = zeros[...]
    in_turn(
        upper_factor(gram_rows, zero, upper),
        solve_rows([normal[8 * k : 8 * k + 8] for k in range(16)], right, zero, solved),
    )
    solved = solved[0]
    factor = jnp.concatenate(upper, axis=0)
    times = lax.dot_general(
        solved, factor, (((1,), (1,)), ((), ())), precision=HIGH
    ) * (2097152.0 ** -0.5)
    t_out[...] = times[0:2]
    columns = jnp.concatenate([solved] * 16, axis=0).T

    def state(blocks, j):
        weights = jnp.broadcast_to(columns[:, j : j + 1], (r, r))
        tiles = []
        for b in range(8):
            tiles.append(jnp.concatenate([
                jnp.sum(get(b * r) * weights, axis=0, keepdims=True) for get in blocks
            ], axis=0))
        return jnp.concatenate(tiles, axis=1)

    own = [functools.partial(lambda k, at: yt[k, :, at : at + r], k) for k in range(8)]
    for half in range(2):
        y_copy(0, half).wait_recv()
        y_copy(1, half).wait_recv()
    h_copy(0).wait_recv()
    h_copy(1).wait_recv()
    outer = [functools.partial(lambda k, at: halo_y[k, :, at : at + r], k) for k in range(2)]
    first, second, edges = state(own, 3), state(own, 2), state(outer, 3)

    coupling = STEP_SIZE * coupling_of(spec[...], rates)
    field = adj[...]
    near = jnp.concatenate([halo[0, 0:1], halo[1, 0:1]], axis=0)
    far = jnp.concatenate([halo[0, 1:2], halo[1, 1:2]], axis=0)
    rate = jnp.concatenate([halo[0, 2:3], halo[1, 2:3]], axis=0) * STEP_SIZE
    inner = jnp.concatenate([field[0:1], field[7:8]], axis=0)
    side = iota((2, WIDTH), 0)
    absent = ((side == 0) & (me == 0)) | ((side == 1) & (me == 255))
    near = jnp.where(absent, 0.0, near)
    near_next = (
        near + DIFFUSION * (far + inner + sideways(near))
        + rate * (1.0 - 3.0 * edges * edges) * near
    )
    near_next = jnp.where(absent, 0.0, near_next)

    def advance(field, low, high, state):
        up = jnp.concatenate([low, field[0:7]], axis=0)
        down = jnp.concatenate([field[1:8], high], axis=0)
        return (
            field + DIFFUSION * (up + down + sideways(field))
            + coupling * (1.0 - 3.0 * state * state) * field
        )

    field = advance(field, near[0:1], near[1:2], first)
    adj_out[...] = advance(field, near_next[0:1], near_next[1:2], second)

    for which in range(2):
        h_copy(which).wait_send()
        y_copy(which, 0).wait_send()
        y_copy(which, 1).wait_send()
    all_of(ar, ar_in, ar_send, ar_recv, PLANE - 1).wait_send()
    all_of(ct_half, ct_in, ct_send, ct_recv, YS * XS - 1).wait_send()
    pair_copy.wait_send()
    all_of(sums, sums, g_send, g_recv, PLANE - 1).wait_send()
    all_of(z_in, z_in, z_send, z_recv, ZS - 1).wait_send()
    all_of(ct_part, ctz_in, cz_send, cz_recv, ZS - 1).wait_send()


def pass_kernel(adj, times, adj_out, times_out):
    adj_out[...] = adj[...]
    times_out[...] = times[...]


def shards(snapshots, range_test, test_rows, species, reaction_rates, adjoint_end):
    vmem = pl.BlockSpec(memory_space=pltpu.VMEM)
    smem = pl.BlockSpec(memory_space=pltpu.SMEM)
    hbm = pl.BlockSpec(memory_space=pl.ANY)
    dma = pltpu.SemaphoreType.DMA
    buffer = pltpu.VMEM
    adjoint, factors = pl.pallas_call(
        whole_kernel,
        in_specs=[hbm, hbm, hbm, hbm, smem, hbm],
        out_specs=[vmem] * 2,
        out_shape=[
            pltpu.VMEM((8, WIDTH), F32),
            pltpu.VMEM((2, 128), F32),
        ],
        scratch_shapes=[
            buffer((STEPS, WIDTH, 512), BF16),
            buffer((STEPS, 256, WIDTH), BF16),
            buffer((512, 128), BF16),
            buffer((8, WIDTH), jnp.int32),
            buffer((8, WIDTH), F32),
            buffer((STEPS, 128, WIDTH), F32),
            buffer((256, 512), F32),
            buffer((128, 256), F32),
            buffer((8, 128), F32),
            buffer((PLANE, 3, 4, 128), F32),
            buffer((2, 16, 16, 256), F32),
            buffer((16, 16, 256), F32),
            buffer((16, 16, 256), F32),
            buffer((PLANE, 3, 4, 128), F32),
            buffer((16, 16, 256), F32),
            buffer((3, 4, 128), F32),
            buffer((ZS, 3, 4, 128), F32),
            buffer((3, 4, 128), F32),
            buffer((PLANE, 3, 4, 128), F32),
            buffer((ZS, 2, 256), F32),
            buffer((ZS, 2, 256), F32),
            buffer((2, 4, WIDTH), F32),
            buffer((2, 4, WIDTH), F32),
            buffer((2, 128, WIDTH), F32),
            dma((STEPS,)), dma((STEPS,)), dma((3,)),
            *([dma] * 10),
            dma((2,)), dma((2,)), dma((4,)), dma((4,)), dma, dma,
        ],
        compiler_params=pltpu.CompilerParams(
            collective_id=0, has_side_effects=True, vmem_limit_bytes=56 << 20
        ),
        name="whole",
    )(snapshots, range_test, test_rows, species, reaction_rates, adjoint_end)
    adjoint, factors = pl.pallas_call(
        pass_kernel,
        in_specs=[vmem] * 2,
        out_specs=[vmem] * 2,
        out_shape=[
            jax.ShapeDtypeStruct((8, WIDTH), F32),
            jax.ShapeDtypeStruct((2, 128), F32),
        ],
        name="pass_on",
    )(
        pltpu.with_memory_space_constraint(adjoint, pltpu.VMEM),
        pltpu.with_memory_space_constraint(factors, pltpu.VMEM),
    )
    return adjoint, factors.T


def solution(mesh):
    cells = ("space", "tm")
    in_specs = (P(cells, None), P(), P(None, cells), P(cells, None), P(), P(cells, None))
    out_specs = (P(cells, None), P(None, cells))
    return jax.shard_map(
        shards, mesh=mesh, in_specs=in_specs, out_specs=out_specs, check_vma=False
    )
```
